256 devices in a mesh: replica: 4 (over z_lo), fsdp: 64 (over y, z_hi, x, core).
Axes of the slice: x: 4, y: 4, z: 8 (z_hi: 2, z_lo: 4; z = z_hi * 4 + z_lo), core: 2. Of those that a mesh axis runs over, the one named last changes fastest.
Arguments:
- tokens: bfloat16 [131072, 8192], P(('replica', 'fsdp')), may hold values from -24 to 24
- cotangent: bfloat16 [131072, 512], P(('replica', 'fsdp')), may hold values from -4 to 4
- z_weights: float32 [8192, 512], P('fsdp'), may hold values from -6 to 6
- x_weights: float32 [8192, 512], P('fsdp'), may hold values from -6 to 6
- second_moment: float32 [8192, 512], P('fsdp'), may hold values from 0.3 to 3
Outputs:
- values: bfloat16 [131072, 512], P(('replica', 'fsdp'))
- z_next: float32 [8192, 512], P('fsdp')
- x_next: float32 [8192, 512], P('fsdp')
- second_next: float32 [8192, 512], P('fsdp')
The draws below stay inside these ranges and needn't reach their ends.
All inputs are finite; a program needn't handle non-finite values.
Results may differ from the reference program's by a relative error of at most 0.0049.
Values may be sent and summed in bfloat16 or wider, within the bound.
A program may use at most 128 MiB of HBM per device.

```python
import math
import jax
import jax.numpy as jnp
from jax import lax

D = 8192
HV = 512
TOK_DEV = 512
TOKENS = 131072


def with_spikes(array, key, source, target, parts, factor):
    owner, partner = [(jnp.arange(array.shape[position]) // (array.shape[position] // parts)).reshape([-1 if axis == position else 1 for axis in range(array.ndim)]) for position in (source, target)]
    chosen = jax.random.permutation(key, parts)[partner]
    strong = (owner == chosen) | (owner == (partner + parts // 2) % parts)
    return jnp.where(strong, factor * array, array)


def levels(key, dims, pieces, low, largest):
    loudness = 1.0
    for axis_at, parts in pieces:
        draws = jax.random.uniform(jax.random.fold_in(jax.random.fold_in(key, 6), axis_at), (parts,), jnp.float32, low / len(pieces), largest / len(pieces))
        loudness = loudness * jnp.repeat(jnp.exp(draws), dims[axis_at] // parts).reshape((-1,) + (1,) * (len(dims) - 1 - axis_at))
    return loudness


def gaussian(own_key, shape, scale, most, cuts=(), kind=jnp.bfloat16):
    entries = scale * jax.random.normal(own_key, shape, jnp.float32)
    if cuts:
        entries = entries * levels(own_key, shape, cuts, -0.22, 0.18)
    return jnp.clip(entries, -most, most).astype(kind)


def noise_with(stream_key, dims, width, limit, cuts, heavy, held_as=jnp.bfloat16):
    array = width * jax.random.normal(stream_key, dims, jnp.float32)
    if cuts:
        array = array * levels(stream_key, dims, cuts, -0.22, 0.18)
    return jnp.clip(with_spikes(array, jax.random.fold_in(stream_key, 3), *heavy), -limit, limit).astype(held_as)


def setup_inputs(seed: int = 0) -> dict:
    streams_of = jax.random.split(jax.random.key(seed), 6)
    tokens = noise_with(streams_of[0], (TOKENS, D), 1.0, 24.0, ((0, 256),), (0, 1, 256, 6.0))
    cotangent = gaussian(streams_of[1], (TOKENS, HV), (D ** 0.5 * TOKENS ** -0.5), 4.0, ((0, 256),))
    z_weights = gaussian(streams_of[2], (D, HV), 1.0, 6.0, ((0, 64),), jnp.float32)
    x_weights = gaussian(streams_of[3], (D, HV), 1.0, 6.0, ((0, 64),), jnp.float32)
    second_moment = jnp.clip(jnp.exp(math.log(3.0) - 2.3025851 * jax.random.uniform(streams_of[4], (D, HV), jnp.float32) ** levels(streams_of[4], (D, HV), ((0, 64),), -0.2, 0.2)), 0.3, 3.0)
    return {"tokens": tokens, "cotangent": cotangent, "z_weights": z_weights, "x_weights": x_weights, "second_moment": second_moment}


beta_first = 0.9
beta_second = 0.95
learn_rate = 0.25
weight_decay = 0.1
step_count = 8.0
epsilon = 1e-08
bias_fix = 1.0 - 0.95 ** 8
mixing = 1.0 / (step_count + 1.0)

def update(gradient, z_weights, x_weights, second_moment, blended):
    second_next = beta_second * second_moment + (1.0 - beta_second) * gradient * gradient
    scaled = gradient / (jnp.sqrt(second_next / bias_fix) + epsilon)
    z_next = z_weights - learn_rate * (scaled + weight_decay * blended)
    x_next = (1.0 - mixing) * x_weights + mixing * z_next
    return (z_next, x_next, second_next)

def reference(tokens, cotangent, z_weights, x_weights, second_moment):
    blended = (1.0 - beta_first) * z_weights + beta_first * x_weights
    weights = blended.astype(jnp.bfloat16)
    widened = weights.astype(jnp.float32)
    norm_factor = 1.0 / math.sqrt(D)
    blocks = tokens.shape[0] // TOK_DEV
    token_blocks = tokens.reshape(blocks, TOK_DEV, D)
    cot_blocks = cotangent.reshape(blocks, TOK_DEV, HV)

    def advance(running, inputs):
        token_block, cot_block = inputs
        block_wide = token_block.astype(jnp.float32)
        outputs = (jnp.dot(block_wide, widened, precision=lax.Precision.HIGHEST) * norm_factor).astype(jnp.bfloat16)
        running = running + jnp.dot(block_wide.T, cot_block.astype(jnp.float32), precision=lax.Precision.HIGHEST) * norm_factor
        return (running, outputs)
    gradient, outputs = lax.scan(advance, jnp.zeros((D, HV), jnp.float32), (token_blocks, cot_blocks))
    values = outputs.reshape(tokens.shape[0], HV)
    z_next, x_next, second_next = update(gradient, z_weights, x_weights, second_moment, blended)
    return (values, z_next, x_next, second_next)
```

```python
import math

import jax
import jax.numpy as jnp
from jax import lax
from jax.experimental import pallas as pl
from jax.experimental.pallas import tpu as pltpu
from jax.sharding import PartitionSpec as P

beta_first = 0.9
beta_second = 0.95
learn_rate = 0.25
weight_decay = 0.1
step_count = 8.0
epsilon = 1e-08
bias_fix = 1.0 - 0.95**8
mixing = 1.0 / (step_count + 1.0)

D = 8192
HV = 512
TOK = 512
NORM = 1.0 / math.sqrt(D)
F32 = jnp.float32
BF16 = jnp.bfloat16
MESH = pl.DeviceIdType.MESH
N_MSG = 84


def kernel(
    tokens, cot_hbm, z_ref, x_ref, s_ref,
    values_out, z_out, x_out, s_out,
    tok, cot, cot_t, wts, gt,
    relay1, direct1, summed1, stage1, g1f, g1b,
    relay2, direct2, summed2, stage2, plane, zstage, zrecv, gfull, acc, vrecv,
    send_sem, recv_sem, tok_local, tok_send, tok_recv, cot_sem,
):
    zl = lax.axis_index("replica")
    index = lax.axis_index("fsdp")
    core = lax.rem(index, 2)
    xc = lax.rem(index // 2, 4)
    zh = lax.rem(index // 8, 2)
    yc = index // 16

    def fsdp_of(y, h, x):
        return ((y * 2 + h) * 4 + x) * 2 + core

    def mod4(v):
        return lax.rem(v + 8, 4)

    partner = (zl, index + 1 - 2 * core)
    x_side = [(zl, fsdp_of(yc, zh, mod4(xc + d))) for d in (1, -1)]
    y_side = [(zl, fsdp_of(mod4(yc + d), zh, xc)) for d in (1, -1)]
    z_now = zh * 4 + zl

    def z_dev(z):
        return (lax.rem(z, 4), fsdp_of(yc, z // 4, xc))

    z_peers = [z_dev(lax.rem(z_now + k, 8)) for k in range(1, 8)]
    mirror = z_dev(7 - z_now)

    barrier = pltpu.get_barrier_semaphore()
    for dev in [partner] + x_side + y_side + z_peers:
        pl.semaphore_signal(barrier, inc=1, device_id=dev, device_id_type=MESH)

    def local_tok(b):
        col = pl.multiple_of((2 * b + core) * 128, 128)
        dst_col = pl.multiple_of(lax.rem(b, 8) * 128, 128)
        return pltpu.make_async_copy(
            tokens.at[:, pl.ds(col, 128)],
            tok.at[b // 8, 0, :, pl.ds(dst_col, 128)],
            tok_local.at[b],
        )

    def remote_tok(b):
        col = pl.multiple_of((2 * b + 1 - core) * 128, 128)
        dst_col = pl.multiple_of(lax.rem(b, 8) * 128, 128)
        return pltpu.make_async_remote_copy(
            src_ref=tokens.at[:, pl.ds(col, 128)],
            dst_ref=tok.at[b // 8, 1, :, pl.ds(dst_col, 128)],
            send_sem=tok_send.at[b],
            recv_sem=tok_recv.at[b],
            device_id=partner,
            device_id_type=MESH,
        )

    cot_local = pltpu.make_async_copy(cot_hbm, cot.at[0], cot_sem)
    cot_local.start()

    @pl.loop(0, 32)
    def _(b):
        local_tok(b).start()

    blended = (1.0 - beta_first) * z_ref[...] + beta_first * x_ref[...]
    wts[yc, zh, xc] = blended.astype(BF16)

    pl.semaphore_wait(barrier, 12)

    sends = []
    counter = [0]

    def message(src, dst, dev):
        m = counter[0]
        counter[0] += 1
        copy = pltpu.make_async_remote_copy(
            src_ref=src, dst_ref=dst, send_sem=send_sem.at[m], recv_sem=recv_sem.at[m],
            device_id=dev, device_id_type=MESH,
        )
        copy.start()
        sends.append(copy)
        return m

    def arrived(m, dst):
        pltpu.make_async_remote_copy(
            src_ref=dst, dst_ref=dst, send_sem=send_sem.at[m], recv_sem=recv_sem.at[m],
            device_id=partner, device_id_type=MESH,
        ).wait_recv()

    first = (xc, yc)
    second = (yc, xc)
    first_side = (x_side, y_side)
    second_side = (y_side, x_side)

    def block(p, f, s, h, r0, rows):
        y, x = (s, f) if p == 0 else (f, s)
        return wts.at[y, h, x, pl.ds(r0, rows), :]

    def line(p, s, h, r0, rows):
        if p == 0:
            return wts.at[s, h, :, pl.ds(r0, rows), :]
        return wts.at[:, h, s, pl.ds(r0, rows), :]

    half_of = (zh, 1 - zh)
    ag = {}

    def ag0(st):
        h = half_of[st]
        for p in (0, 1):
            f, s, r0 = first[p], second[p], 64 * p
            own = block(p, f, s, h, r0, 64)
            for d in (0, 1):
                ag[st, p, 0, d] = message(own, own, first_side[p][d])

    def ag1(st):
        h = half_of[st]
        for p in (0, 1):
            f, s, r0 = first[p], second[p], 64 * p
            for d in (0, 1):
                src_f = mod4(f - 1 + 2 * d)
                arrived(ag[st, p, 0, d], block(p, src_f, s, h, r0, 64))
                part = block(p, src_f, s, h, r0 + 32 * d, 32)
                ag[st, p, 1, d] = message(part, part, first_side[p][d])

    def ag2(st):
        h = half_of[st]
        for p in (0, 1):
            f, s, r0 = first[p], second[p], 64 * p
            for d in (0, 1):
                arrived(ag[st, p, 1, d], block(p, mod4(f + 2), s, h, r0 + 32 * d, 32))
            row = line(p, s, h, r0, 64)
            for d in (0, 1):
                ag[st, p, 2, d] = message(row, row, second_side[p][d])

    def ag3(st):
        h = half_of[st]
        for p in (0, 1):
            s, r0 = second[p], 64 * p
            for d in (0, 1):
                src_s = mod4(s - 1 + 2 * d)
                arrived(ag[st, p, 2, d], line(p, src_s, h, r0, 64))
                part = line(p, src_s, h, r0 + 32 * d, 32)
                ag[st, p, 3, d] = message(part, part, second_side[p][d])

    def ag4(st):
        h = half_of[st]
        for p in (0, 1):
            s, r0 = second[p], 64 * p
            for d in (0, 1):
                arrived(ag[st, p, 3, d], line(p, mod4(s + 2), h, r0 + 32 * d, 32))

    cot_msg = message(cot_hbm, cot.at[1], partner)
    ag0(0)
    own = wts.at[yc, zh, xc]
    mirror_msg = message(own, own, mirror)

    @pl.loop(0, 32)
    def _(b):
        remote_tok(b).start()

    cot_local.wait()
    arrived(cot_msg, cot.at[1])
    for k in (0, 1):
        cot_t[:, 512 * k:512 * (k + 1)] = cot[k].T

    def grad_step(j):
        for b in (2 * j, 2 * j + 1):
            local_tok(b).wait()
            remote_tok(b).wait_recv()
        y, h, pair = j // 4, lax.rem(j // 2, 2), lax.rem(j, 2)
        col = pl.multiple_of(lax.rem(j, 4) * 256, 256)
        rhs = tok[y, :, :, pl.ds(col, 256)].reshape(1024, 256)
        for q in (0, 1):
            out = jnp.dot(cot_t[256 * q:256 * (q + 1), :], rhs, preferred_element_type=F32).astype(BF16)
            gt[y, h, 2 * pair, 256 * q:256 * (q + 1), :] = out[:, :128]
            gt[y, h, 2 * pair + 1, 256 * q:256 * (q + 1), :] = out[:, 128:]

    def grad(j0, j1):
        @pl.loop(j0, j1)
        def _(j):
            grad_step(j)

    ag1(0)
    grad(0, 2)
    arrived(mirror_msg, wts.at[yc, 1 - zh, xc])
    ag0(1)
    ag2(0)
    grad(2, 5)
    ag1(1)
    grad(5, 8)
    ag2(1)
    grad(8, 12)
    ag3(0)
    grad(12, 16)

    def gset(p, f, h):
        hv = pl.ds(256 * p, 256)
        if p == 0:
            return gt.at[:, h, f, hv, :]
        return gt.at[f, h, :, hv, :]

    def gblk(p, f, h, i):
        hv = pl.ds(256 * p, 256)
        if p == 0:
            return gt[i, h, f, hv, :].astype(F32)
        return gt[f, h, i, hv, :].astype(F32)

    def nxt(c, d):
        return mod4(c + 1 - 2 * d)

    rs = {}
    for p in (0, 1):
        for d in (0, 1):
            rs[p, 0, d] = message(gset(p, mod4(first[p] + 2), d), relay1.at[p, d], first_side[p][d])
    for p in (0, 1):
        for d in (0, 1):
            rs[p, 1, d] = message(gset(p, nxt(first[p], d), 1 - d), direct1.at[p, d], first_side[p][d])

    ag3(1)
    ag4(0)

    acc_first = [True]

    def values_step(y, m):
        lhs = tok[y, m]
        rhs = wts[y].reshape(1024, 512)
        acc[m] += jnp.dot(lhs, rhs, preferred_element_type=F32)

    acc[...] = jnp.zeros_like(acc)

    def rs1_c():
        for p in (0, 1):
            for d in (0, 1):
                arrived(rs[p, 0, d], relay1.at[p, d])

                @pl.loop(0, 4)
                def _(i):
                    stage1[p, d, i] = (gblk(p, nxt(first[p], d), d, i) + relay1[p, d, i].astype(F32)).astype(BF16)

                rs[p, 2, d] = message(stage1.at[p, d], summed1.at[p, d], first_side[p][d])

    rs1_c()
    ag4(1)

    def values(y0, y1):
        @pl.loop(y0, y1)
        def _(y):
            @pl.loop(0, 2)
            def _(m):
                values_step(y, m)

    values(0, 2)

    for p in (0, 1):
        for d in (0, 1):
            arrived(rs[p, 1, d], direct1.at[p, d])
            arrived(rs[p, 2, d], summed1.at[p, d])
        for h in (0, 1):
            @pl.loop(0, 4)
            def _(i):
                total = (
                    gblk(p, first[p], h, i)
                    + direct1[p, 1 - h, i].astype(F32)
                    + summed1[p, h, i].astype(F32)
                )
                g1f[p, i, h] = total
                g1b[p, i, h] = total.astype(BF16)
        s = second[p]
        for d in (0, 1):
            rs[p, 3, d] = message(g1b.at[p, mod4(s + 2), d], relay2.at[p, d], second_side[p][d])
        for d in (0, 1):
            rs[p, 4, d] = message(g1b.at[p, nxt(s, d), 1 - d], direct2.at[p, d], second_side[p][d])

    values(2, 4)
    vmsg = message(acc.at[1], vrecv, partner)

    for p in (0, 1):
        for d in (0, 1):
            arrived(rs[p, 3, d], relay2.at[p, d])
            stage2[p, d] = (g1f[p, nxt(second[p], d), d] + relay2[p, d].astype(F32)).astype(BF16)
            rs[p, 5, d] = message(stage2.at[p, d], summed2.at[p, d], second_side[p][d])

    for p in (0, 1):
        for d in (0, 1):
            arrived(rs[p, 4, d], direct2.at[p, d])
            arrived(rs[p, 5, d], summed2.at[p, d])
        for h in (0, 1):
            total = g1f[p, second[p], h] + direct2[p, 1 - h].astype(F32) + summed2[p, h].astype(F32)
            plane[h, 256 * p:256 * (p + 1), :] = total
            zstage[h, 256 * p:256 * (p + 1), :] = total.astype(BF16)

    zmsgs = []
    for k in range(1, 8):
        dest = lax.rem(z_now + k, 8)
        piece = zstage.at[dest // 4, pl.ds(pl.multiple_of(lax.rem(dest, 4) * 128, 128), 128), :]
        zmsgs.append(message(piece, zrecv.at[k - 1], z_peers[k - 1]))

    arrived(vmsg, vrecv)
    values_out[...] = ((acc[0] + vrecv[...]) * NORM).astype(BF16)

    my_hv = pl.ds(pl.multiple_of(zl * 128, 128), 128)
    total = plane[zh, my_hv, :]
    for k in range(7):
        arrived(zmsgs[k], zrecv.at[k])
        total = total + zrecv[k].astype(F32)
    gfull[my_hv, :] = total
    rmsgs = []
    for k in range(1, 4):
        rmsgs.append(message(gfull.at[my_hv, :], gfull.at[my_hv, :], (lax.rem(zl + k, 4), index)))
    for k in range(1, 4):
        src = pl.multiple_of(lax.rem(zl + 4 - k, 4) * 128, 128)
        arrived(rmsgs[k - 1], gfull.at[pl.ds(src, 128), :])

    gradient = gfull[...].T * NORM
    z_in = z_ref[...]
    x_in = x_ref[...]
    mixed = (1.0 - beta_first) * z_in + beta_first * x_in
    second_next = beta_second * s_ref[...] + (1.0 - beta_second) * gradient * gradient
    scaled = gradient / (jnp.sqrt(second_next / bias_fix) + epsilon)
    z_next = z_in - learn_rate * (scaled + weight_decay * mixed)
    s_out[...] = second_next
    z_out[...] = z_next
    x_out[...] = (1.0 - mixing) * x_in + mixing * z_next

    for copy in sends:
        copy.wait_send()

    @pl.loop(0, 32)
    def _(b):
        remote_tok(b).wait_send()

    assert counter[0] <= N_MSG


def local(tokens, cotangent, z_weights, x_weights, second_moment):
    vm = pl.BlockSpec(memory_space=pltpu.VMEM)
    hbm = pl.BlockSpec(memory_space=pl.ANY)
    shard = jax.ShapeDtypeStruct((128, HV), F32)
    dma = pltpu.SemaphoreType.DMA
    return pl.pallas_call(
        kernel,
        out_shape=(jax.ShapeDtypeStruct((TOK, HV), BF16), shard, shard, shard),
        in_specs=[hbm, hbm, vm, vm, vm],
        out_specs=(vm, vm, vm, vm),
        scratch_shapes=[
            pltpu.VMEM((4, 2, 512, 1024), BF16),
            pltpu.VMEM((2, 512, 512), BF16),
            pltpu.VMEM((512, 1024), BF16),
            pltpu.VMEM((4, 2, 4, 128, 512), BF16),
            pltpu.VMEM((4, 2, 4, 512, 128), BF16),
            pltpu.VMEM((2, 2, 4, 256, 128), BF16),
            pltpu.VMEM((2, 2, 4, 256, 128), BF16),
            pltpu.VMEM((2, 2, 4, 256, 128), BF16),
            pltpu.VMEM((2, 2, 4, 256, 128), BF16),
            pltpu.VMEM((2, 4, 2, 256, 128), F32),
            pltpu.VMEM((2, 4, 2, 256, 128), BF16),
            pltpu.VMEM((2, 2, 256, 128), BF16),
            pltpu.VMEM((2, 2, 256, 128), BF16),
            pltpu.VMEM((2, 2, 256, 128), BF16),
            pltpu.VMEM((2, 2, 256, 128), BF16),
            pltpu.VMEM((2, 512, 128), F32),
            pltpu.VMEM((2, 512, 128), BF16),
            pltpu.VMEM((7, 128, 128), BF16),
            pltpu.VMEM((512, 128), F32),
            pltpu.VMEM((2, 512, 512), F32),
            pltpu.VMEM((512, 512), F32),
            dma((N_MSG,)),
            dma((N_MSG,)),
            dma((32,)),
            dma((32,)),
            dma((32,)),
            dma,
        ],
        compiler_params=pltpu.CompilerParams(
            collective_id=0, has_side_effects=True, vmem_limit_bytes=56 * 1024 * 1024
        ),
    )(tokens, cotangent, z_weights, x_weights, second_moment)


def solution(mesh):
    return jax.shard_map(
        local,
        mesh=mesh,
        in_specs=(
            P(("replica", "fsdp"), None),
            P(("replica", "fsdp"), None),
            P("fsdp", None),
            P("fsdp", None),
            P("fsdp", None),
        ),
        out_specs=(P(("replica", "fsdp"), None), P("fsdp", None), P("fsdp", None), P("fsdp", None)),
        check_vma=False,
    )
```

```python
import math

import jax
import jax.numpy as jnp
from jax import lax
from jax.experimental import pallas as pl
from jax.experimental.pallas import tpu as pltpu
from jax.sharding import PartitionSpec as P

beta_first = 0.9
beta_second = 0.95
learn_rate = 0.25
weight_decay = 0.1
step_count = 8.0
epsilon = 1e-08
bias_fix = 1.0 - 0.95**8
mixing = 1.0 / (step_count + 1.0)

D = 8192
HV = 512
TOK = 512
NORM = 1.0 / math.sqrt(D)
F32 = jnp.float32
BF16 = jnp.bfloat16
MESH = pl.DeviceIdType.MESH
N_MSG = 176


def kernel(
    tokens, cot_hbm, z_hbm, x_hbm,
    values_out, grad_out,
    z_ref, x_ref, tok, cot, cot_t, wts, gt,
    relay1, direct1, summed1, stage1, g1f, g1b, relay2, direct2, summed2, stage2,
    c_f, c_b,
    c_relay1, c_direct1, c_summed1, c_stage1, c_g1f, c_g1b, c_relay2, c_direct2, c_summed2, c_stage2,
    zc_half, zc_recv, zc_stage,
    plane, zstage, zrecv, gfull, acc, vrecv,
    send_sem, recv_sem, tok_local, tok_send, tok_recv, in_sem,
):
    zl = lax.axis_index("replica")
    index = lax.axis_index("fsdp")
    core = lax.rem(index, 2)
    xc = lax.rem(index // 2, 4)
    zh = lax.rem(index // 8, 2)
    yc = index // 16

    def fsdp_of(y, h, x):
        return ((y * 2 + h) * 4 + x) * 2 + core

    def mod4(v):
        return lax.rem(v + 8, 4)

    partner = (zl, index + 1 - 2 * core)
    x_side = [(zl, fsdp_of(yc, zh, mod4(xc + d))) for d in (1, -1)]
    y_side = [(zl, fsdp_of(mod4(yc + d), zh, xc)) for d in (1, -1)]
    z_now = zh * 4 + zl

    def z_plus(k):
        return lax.rem(z_now + k + 8, 8)

    def z_dev(z):
        return (lax.rem(z, 4), fsdp_of(yc, z // 4, xc))

    z_peers = [z_dev(z_plus(k)) for k in range(1, 8)]
    z_side = [z_dev(z_plus(1)), z_dev(z_plus(-1))]
    mirror = z_dev(7 - z_now)

    barrier = pltpu.get_barrier_semaphore()
    for dev in [partner] + x_side + y_side + z_peers:
        pl.semaphore_signal(barrier, inc=1, device_id=dev, device_id_type=MESH)

    def place(t):
        h = lax.rem(1 - zh + t // 16, 2)
        return lax.rem(t // 4, 4), h, lax.rem(t, 4)

    def tok_cols(t, side):
        y, h, x = place(t)
        src = pl.multiple_of((2 * ((y * 2 + h) * 4 + x) + side) * 128, 128)
        dst = pl.multiple_of((h * 4 + x) * 128, 128)
        return y, src, dst

    def local_tok(t):
        y, src, dst = tok_cols(t, core)
        return pltpu.make_async_copy(
            tokens.at[:, pl.ds(src, 128)], tok.at[y, 0, :, pl.ds(dst, 128)], tok_local.at[t]
        )

    def remote_tok(t):
        y, src, dst = tok_cols(t, 1 - core)
        return pltpu.make_async_remote_copy(
            src_ref=tokens.at[:, pl.ds(src, 128)],
            dst_ref=tok.at[y, 1, :, pl.ds(dst, 128)],
            send_sem=tok_send.at[t],
            recv_sem=tok_recv.at[t],
            device_id=partner,
            device_id_type=MESH,
        )

    z_in = pltpu.make_async_copy(z_hbm, z_ref, in_sem.at[0])
    x_in = pltpu.make_async_copy(x_hbm, x_ref, in_sem.at[1])
    cot_local = pltpu.make_async_copy(cot_hbm, cot.at[0], in_sem.at[2])
    z_in.start()
    x_in.start()
    cot_local.start()

    @pl.loop(0, 32)
    def _(t):
        local_tok(t).start()

    z_in.wait()
    x_in.wait()
    blended = (1.0 - beta_first) * z_ref[...] + beta_first * x_ref[...]
    wts[yc, zh, xc] = blended.astype(BF16)

    pl.semaphore_wait(barrier, 12)

    sends = []
    counter = [0]

    def message(src, dst, dev):
        m = counter[0]
        counter[0] += 1
        copy = pltpu.make_async_remote_copy(
            src_ref=src, dst_ref=dst, send_sem=send_sem.at[m], recv_sem=recv_sem.at[m],
            device_id=dev, device_id_type=MESH,
        )
        copy.start()
        sends.append(copy)
        return m

    def arrived(m, dst):
        pltpu.make_async_remote_copy(
            src_ref=dst, dst_ref=dst, send_sem=send_sem.at[m], recv_sem=recv_sem.at[m],
            device_id=partner, device_id_type=MESH,
        ).wait_recv()

    first = (xc, yc)
    second = (yc, xc)
    first_side = (x_side, y_side)
    second_side = (y_side, x_side)

    def block(p, f, s, h, r0, rows):
        y, x = (s, f) if p == 0 else (f, s)
        return wts.at[y, h, x, pl.ds(r0, rows), :]

    half_of = (zh, 1 - zh)
    ag = {}

    def spread(st, p, item):
        h = half_of[st]
        blk = block(p, mod4(first[p] + item), second[p], h, 64 * p, 64)
        for d in (0, 1):
            ag[st, p, 2, item, d] = message(blk, blk, second_side[p][d])

    def ag0(st):
        h = half_of[st]
        for p in (0, 1):
            own = block(p, first[p], second[p], h, 64 * p, 64)
            for d in (0, 1):
                ag[st, p, 0, d] = message(own, own, first_side[p][d])
        for p in (0, 1):
            spread(st, p, 0)

    def ag1(st):
        h = half_of[st]
        for p in (0, 1):
            f, s, r0 = first[p], second[p], 64 * p
            for d in (0, 1):
                src_f = mod4(f - 1 + 2 * d)
                arrived(ag[st, p, 0, d], block(p, src_f, s, h, r0, 64))
                part = block(p, src_f, s, h, r0 + 32 * d, 32)
                ag[st, p, 1, d] = message(part, part, first_side[p][d])
                spread(st, p, -1 + 2 * d)

    def ag2(st):
        h = half_of[st]
        for p in (0, 1):
            f, s, r0 = first[p], second[p], 64 * p
            for d in (0, 1):
                arrived(ag[st, p, 1, d], block(p, mod4(f + 2), s, h, r0 + 32 * d, 32))
            spread(st, p, 2)

    def ag3(st, items):
        h = half_of[st]
        for item in items:
            for p in (0, 1):
                f, s, r0 = first[p], second[p], 64 * p
                for d in (0, 1):
                    src_s = mod4(s - 1 + 2 * d)
                    arrived(ag[st, p, 2, item, d], block(p, mod4(f + item), src_s, h, r0, 64))
                    part = block(p, mod4(f + item), src_s, h, r0 + 32 * d, 32)
                    ag[st, p, 3, item, d] = message(part, part, second_side[p][d])

    def ag4(st):
        h = half_of[st]
        for item in (0, -1, 1, 2):
            for p in (0, 1):
                f, s, r0 = first[p], second[p], 64 * p
                for d in (0, 1):
                    arrived(ag[st, p, 3, item, d], block(p, mod4(f + item), mod4(s + 2), h, r0 + 32 * d, 32))

    zc = {}

    def piece(z, c, r0, rows):
        row = pl.multiple_of(lax.rem(z, 4) * 64 + r0, 32)
        return gt.at[pl.ds(2 * c, 2), z // 4, :, pl.ds(row, rows), :]

    def zc1(c):
        dest = z_plus(4)
        for d in (0, 1):
            zc[1, d, c] = message(piece(dest, c, 32 * d, 32), zc_half.at[d, c], z_side[d])

    def zc_step(s, c):
        for d in (0, 1):
            dest = z_plus((5 - s) * (1 - 2 * d))
            h = dest // 4
            row = pl.multiple_of(lax.rem(dest, 4) * 64, 64)
            if s == 2:
                arrived(zc[1, d, c], zc_half.at[d, c])
            else:
                arrived(zc[s - 1, d, c], zc_recv.at[s - 3, d, c])

            @pl.loop(0, 8)
            def _(i):
                y, x = i // 4, lax.rem(i, 4)
                mine = gt[2 * c + y, h, x, pl.ds(row, 64), :]
                if s == 2:
                    a, b = 32 * d, 32 - 32 * d
                    got = zc_half[d, c, y, x].astype(F32)
                    zc_stage[0, d, c, y, x, a:a + 32, :] = (mine[a:a + 32, :].astype(F32) + got).astype(BF16)
                    zc_stage[0, d, c, y, x, b:b + 32, :] = mine[b:b + 32, :]
                else:
                    got = zc_recv[s - 3, d, c, y, x].astype(F32)
                    zc_stage[s - 2, d, c, y, x] = (mine.astype(F32) + got).astype(BF16)

            zc[s, d, c] = message(zc_stage.at[s - 2, d, c], zc_recv.at[s - 2, d, c], z_side[d])

    def zc_final(c):
        for d in (0, 1):
            arrived(zc[4, d, c], zc_recv.at[2, d, c])
        row = pl.multiple_of(zl * 64, 64)

        @pl.loop(0, 8)
        def _(i):
            y, x = i // 4, lax.rem(i, 4)
            total = (
                gt[2 * c + y, zh, x, pl.ds(row, 64), :].astype(F32)
                + zc_recv[2, 0, c, y, x].astype(F32)
                + zc_recv[2, 1, c, y, x].astype(F32)
            )
            for p in (0, 1):
                for k in (0, 1):
                    part = total[32 * p + 16 * k:32 * p + 16 * k + 16, :]
                    c_f[p, 2 * c + y, k, x] = part
                    c_b[p, 2 * c + y, k, x] = part.astype(BF16)

    def nxt(c, d):
        return mod4(c + 1 - 2 * d)

    class Plane:
        def __init__(self, pick, load, bufs):
            self.pick, self.load, self.bufs, self.m = pick, load, bufs, {}

        def start(self, p, which):
            rel, dirc = self.bufs[0], self.bufs[1]
            for d in (0, 1):
                if which == 0:
                    src, dst = self.pick(p, mod4(first[p] + 2), d), rel.at[p, d]
                else:
                    src, dst = self.pick(p, nxt(first[p], d), 1 - d), dirc.at[p, d]
                self.m[p, which, d] = message(src, dst, first_side[p][d])

        def mid(self, p):
            rel, _, summed, stage = self.bufs[:4]
            for d in (0, 1):
                arrived(self.m[p, 0, d], rel.at[p, d])

                @pl.loop(0, 4)
                def _(i):
                    stage[p, d, i] = (self.load(p, nxt(first[p], d), d, i) + rel[p, d, i].astype(F32)).astype(BF16)

                self.m[p, 2, d] = message(stage.at[p, d], summed.at[p, d], first_side[p][d])

        def turn(self, p):
            _, dirc, summed, _, gf, gb, rel2, dir2 = self.bufs[:8]
            for d in (0, 1):
                arrived(self.m[p, 1, d], dirc.at[p, d])
                arrived(self.m[p, 2, d], summed.at[p, d])
            for h in (0, 1):
                @pl.loop(0, 4)
                def _(i):
                    total = (
                        self.load(p, first[p], h, i)
                        + dirc[p, 1 - h, i].astype(F32)
                        + summed[p, h, i].astype(F32)
                    )
                    gf[p, i, h] = total
                    gb[p, i, h] = total.astype(BF16)
            s = second[p]
            for d in (0, 1):
                self.m[p, 3, d] = message(gb.at[p, mod4(s + 2), d], rel2.at[p, d], second_side[p][d])
            for d in (0, 1):
                self.m[p, 4, d] = message(gb.at[p, nxt(s, d), 1 - d], dir2.at[p, d], second_side[p][d])

        def mid2(self, p):
            gf, _, rel2, _, summed2, stage2_ = self.bufs[4:]
            for d in (0, 1):
                arrived(self.m[p, 3, d], rel2.at[p, d])
                stage2_[p, d] = (gf[p, nxt(second[p], d), d] + rel2[p, d].astype(F32)).astype(BF16)
                self.m[p, 5, d] = message(stage2_.at[p, d], summed2.at[p, d], second_side[p][d])

        def end(self, p):
            gf, _, _, dir2, summed2, _ = self.bufs[4:]
            for d in (0, 1):
                arrived(self.m[p, 4, d], dir2.at[p, d])
                arrived(self.m[p, 5, d], summed2.at[p, d])
            return [
                gf[p, second[p], h] + dir2[p, 1 - h].astype(F32) + summed2[p, h].astype(F32)
                for h in (0, 1)
            ]

    def ab_pick(p, f, h):
        rows = pl.ds(256 + 128 * p, 128)
        return gt.at[:, h, f, rows, :] if p == 0 else gt.at[f, h, :, rows, :]

    def ab_load(p, f, h, i):
        rows = pl.ds(256 + 128 * p, 128)
        return (gt[i, h, f, rows, :] if p == 0 else gt[f, h, i, rows, :]).astype(F32)

    def c_pick(p, f, h):
        return c_b.at[0, :, h, f] if p == 0 else c_b.at[1, f, h]

    def c_load(p, f, h, i):
        return c_f[0, i, h, f] if p == 0 else c_f[1, f, h, i]

    ab = Plane(ab_pick, ab_load, (relay1, direct1, summed1, stage1, g1f, g1b, relay2, direct2, summed2, stage2))
    cc = Plane(
        c_pick, c_load,
        (c_relay1, c_direct1, c_summed1, c_stage1, c_g1f, c_g1b, c_relay2, c_direct2, c_summed2, c_stage2),
    )

    def grad(j0, j1):
        @pl.loop(j0, j1)
        def _(j):
            for t in (2 * j, 2 * j + 1):
                local_tok(t).wait()
                remote_tok(t).wait_recv()
            y, h, x = place(2 * j)
            col = pl.multiple_of(h * 512 + x * 128, 256)
            rhs = tok[y, :, :, pl.ds(col, 256)].reshape(1024, 256)
            for q in (0, 1):
                rows = slice(256 * q, 256 * (q + 1))
                out = jnp.dot(cot_t[rows, :], rhs, preferred_element_type=F32).astype(BF16)
                gt[y, h, x, rows, :] = out[:, :128]
                gt[y, h, x + 1, rows, :] = out[:, 128:]

    def values(y):
        @pl.loop(0, 2)
        def _(m):
            out = jnp.dot(tok[y, m], wts[y].reshape(1024, 512), preferred_element_type=F32)
            acc[m] = out if y == 0 else acc[m] + out

    cot_msg = message(cot_hbm, cot.at[1], partner)
    ag0(0)
    own = wts.at[yc, zh, xc]
    mirror_msg = message(own, own, mirror)

    @pl.loop(0, 32)
    def _(t):
        remote_tok(t).start()

    cot_local.wait()
    arrived(cot_msg, cot.at[1])
    for k in (0, 1):
        cot_t[:, 512 * k:512 * (k + 1)] = cot[k].T

    ag1(0)
    grad(0, 2)
    ag2(0)
    grad(2, 4)
    zc1(0)
    arrived(mirror_msg, wts.at[yc, 1 - zh, xc])
    ag0(1)
    grad(4, 6)
    ag3(0, (0,))
    grad(6, 8)
    zc1(1)
    ag1(1)
    grad(8, 12)
    ag3(0, (-1, 1))
    ag2(1)
    grad(12, 16)
    zc_step(2, 0)
    for p in (0, 1):
        ab.start(p, 0)
    ag3(0, (2,))
    ag3(1, (0,))
    zc_step(2, 1)
    ag3(1, (-1, 1))
    zc_step(3, 0)
    for p in (0, 1):
        ab.start(p, 1)
    ag3(1, (2,))
    ag4(0)
    zc_step(3, 1)
    for p in (0, 1):
        ab.mid(p)
    zc_step(4, 0)
    ag4(1)
    values(0)
    zc_step(4, 1)
    values(1)
    for p in (0, 1):
        ab.turn(p)
    zc_final(0)
    zc_final(1)
    for p in (0, 1):
        cc.start(p, 0)
        cc.start(p, 1)
    values(2)
    for p in (0, 1):
        ab.mid2(p)
        cc.mid(p)
    values(3)
    vmsg = message(acc.at[1], vrecv, partner)
    for p in (0, 1):
        cc.turn(p)
    for p in (0, 1):
        for h, total in enumerate(ab.end(p)):
            plane[h, 128 * p:128 * (p + 1), :] = total
            zstage[h, 128 * p:128 * (p + 1), :] = total.astype(BF16)

    zmsgs = []
    for k in range(1, 8):
        dest = z_plus(k)
        part = zstage.at[dest // 4, pl.ds(pl.multiple_of(lax.rem(dest, 4) * 64, 64), 64), :]
        zmsgs.append(message(part, zrecv.at[k - 1], z_peers[k - 1]))

    for p in (0, 1):
        cc.mid2(p)

    def share(base):
        rows = gfull.at[pl.ds(pl.multiple_of(base + zl * 64, 64), 64), :]
        return [message(rows, rows, (lax.rem(zl + k, 4), index)) for k in range(1, 4)]

    def shared(base, msgs):
        for k in range(1, 4):
            row = pl.multiple_of(base + lax.rem(zl + 4 - k, 4) * 64, 64)
            arrived(msgs[k - 1], gfull.at[pl.ds(row, 64), :])

    my_rows = pl.ds(pl.multiple_of(zl * 64, 64), 64)
    for p in (0, 1):
        for h, total in enumerate(cc.end(p)):
            gfull[pl.ds(pl.multiple_of(zl * 64 + 32 * p + 16 * h, 16), 16), :] = total
    c_msgs = share(0)

    total = plane[zh, my_rows, :]
    for k in range(7):
        arrived(zmsgs[k], zrecv.at[k])
        total = total + zrecv[k].astype(F32)
    gfull[pl.ds(pl.multiple_of(256 + zl * 64, 64), 64), :] = total
    ab_msgs = share(256)

    arrived(vmsg, vrecv)
    values_out[...] = ((acc[0] + vrecv[...]) * NORM).astype(BF16)

    shared(0, c_msgs)
    shared(256, ab_msgs)
    grad_out[...] = gfull[...]

    for copy in sends:
        copy.wait_send()

    @pl.loop(0, 32)
    def _(t):
        remote_tok(t).wait_send()

    assert counter[0] <= N_MSG


def finish(values_ref, grad_ref, z_ref, x_ref, s_ref, values_out, z_out, x_out, s_out):
    values_out[...] = values_ref[...]
    gradient = grad_ref[...].T * NORM
    z_in = z_ref[...]
    x_in = x_ref[...]
    mixed = (1.0 - beta_first) * z_in + beta_first * x_in
    second_next = beta_second * s_ref[...] + (1.0 - beta_second) * gradient * gradient
    scaled = gradient / (jnp.sqrt(second_next / bias_fix) + epsilon)
    z_next = z_in - learn_rate * (scaled + weight_decay * mixed)
    s_out[...] = second_next
    z_out[...] = z_next
    x_out[...] = (1.0 - mixing) * x_in + mixing * z_next


def local(tokens, cotangent, z_weights, x_weights, second_moment):
    vm = pl.BlockSpec(memory_space=pltpu.VMEM)
    hbm = pl.BlockSpec(memory_space=pl.ANY)
    shard = jax.ShapeDtypeStruct((128, HV), F32)
    vals = jax.ShapeDtypeStruct((TOK, HV), BF16)
    dma = pltpu.SemaphoreType.DMA

    def plane_bufs(r):
        return (
            [pltpu.VMEM((2, 2, 4, r, 128), BF16)] * 4
            + [pltpu.VMEM((2, 4, 2, r, 128), F32), pltpu.VMEM((2, 4, 2, r, 128), BF16)]
            + [pltpu.VMEM((2, 2, r, 128), BF16)] * 4
        )

    values, gradient = pl.pallas_call(
        kernel,
        out_shape=(vals, jax.ShapeDtypeStruct((HV, 128), F32)),
        in_specs=[hbm, hbm, hbm, hbm],
        out_specs=(vm, vm),
        scratch_shapes=[
            pltpu.VMEM((128, HV), F32),
            pltpu.VMEM((128, HV), F32),
            pltpu.VMEM((4, 2, 512, 1024), BF16),
            pltpu.VMEM((2, 512, 512), BF16),
            pltpu.VMEM((512, 1024), BF16),
            pltpu.VMEM((4, 2, 4, 128, 512), BF16),
            pltpu.VMEM((4, 2, 4, 512, 128), BF16),
        ] + plane_bufs(128) + [
            pltpu.VMEM((2, 4, 2, 4, 16, 128), F32),
            pltpu.VMEM((2, 4, 2, 4, 16, 128), BF16),
        ] + plane_bufs(16) + [
            pltpu.VMEM((2, 2, 2, 4, 32, 128), BF16),
            pltpu.VMEM((3, 2, 2, 2, 4, 64, 128), BF16),
            pltpu.VMEM((3, 2, 2, 2, 4, 64, 128), BF16),
            pltpu.VMEM((2, 256, 128), F32),
            pltpu.VMEM((2, 256, 128), BF16),
            pltpu.VMEM((7, 64, 128), BF16),
            pltpu.VMEM((512, 128), F32),
            pltpu.VMEM((2, 512, 512), F32),
            pltpu.VMEM((512, 512), F32),
            dma((N_MSG,)),
            dma((N_MSG,)),
            dma((32,)),
            dma((32,)),
            dma((32,)),
            dma((3,)),
        ],
        compiler_params=pltpu.CompilerParams(
            collective_id=0, has_side_effects=True, vmem_limit_bytes=48 * 1024 * 1024
        ),
    )(tokens, cotangent, z_weights, x_weights)
    return pl.pallas_call(
        finish,
        out_shape=(vals, shard, shard, shard),
        in_specs=[vm] * 5,
        out_specs=(vm,) * 4,
        compiler_params=pltpu.CompilerParams(vmem_limit_bytes=12 * 1024 * 1024),
    )(values, gradient, z_weights, x_weights, second_moment)


def solution(mesh):
    return jax.shard_map(
        local,
        mesh=mesh,
        in_specs=(
            P(("replica", "fsdp"), None),
            P(("replica", "fsdp"), None),
            P("fsdp", None),
            P("fsdp", None),
            P("fsdp", None),
        ),
        out_specs=(P(("replica", "fsdp"), None), P("fsdp", None), P("fsdp", None), P("fsdp", None)),
        check_vma=False,
    )
```

```python
import math

import jax
import jax.numpy as jnp
from jax import lax
from jax.experimental import pallas as pl
from jax.experimental.pallas import tpu as pltpu
from jax.sharding import PartitionSpec as P

beta_first = 0.9
beta_second = 0.95
learn_rate = 0.25
weight_decay = 0.1
step_count = 8.0
epsilon = 1e-08
bias_fix = 1.0 - 0.95**8
mixing = 1.0 / (step_count + 1.0)

D = 8192
HV = 512
TOK = 512
NORM = 1.0 / math.sqrt(D)
F32 = jnp.float32
BF16 = jnp.bfloat16
MESH = pl.DeviceIdType.MESH
N_MSG = 160
C_ROWS = 80
AB = 4 * C_ROWS
R = (HV - AB) // 2
Q = R // 2


def kernel(
    tokens, cot_hbm, z_hbm, x_hbm,
    values_out, grad_out,
    z_ref, x_ref, tok, cot, cot_t, wts, gt,
    relay1, direct1, summed1, stage1, g1f, g1b, relay2, direct2, summed2, stage2,
    c_f, c_b, c_recv,
    zc_half, zc_recv, zc_stage,
    plane, zstage, zrecv, gfull, acc, vrecv,
    send_sem, recv_sem, tok_local, tok_send, tok_recv, in_sem,
):
    zl = lax.axis_index("replica")
    index = lax.axis_index("fsdp")
    core = lax.rem(index, 2)
    xc = lax.rem(index // 2, 4)
    zh = lax.rem(index // 8, 2)
    yc = index // 16

    def fsdp_of(y, h, x):
        return ((y * 2 + h) * 4 + x) * 2 + core

    def mod4(v):
        return lax.rem(v + 8, 4)

    partner = (zl, index + 1 - 2 * core)
    x_side = [(zl, fsdp_of(yc, zh, mod4(xc + d))) for d in (1, -1)]
    y_side = [(zl, fsdp_of(mod4(yc + d), zh, xc)) for d in (1, -1)]
    z_now = zh * 4 + zl

    def z_plus(k):
        return lax.rem(z_now + k + 8, 8)

    def z_dev(z):
        return (lax.rem(z, 4), fsdp_of(yc, z // 4, xc))

    z_peers = [z_dev(z_plus(k)) for k in range(1, 8)]
    z_side = [z_dev(z_plus(1)), z_dev(z_plus(-1))]
    mirror = z_dev(7 - z_now)

    def plane_plus(k):
        return lax.rem(yc * 4 + xc + k, 16)

    def plane_dev(i):
        return (zl, fsdp_of(i // 4, zh, lax.rem(i, 4)))

    plane_peers = [plane_dev(plane_plus(k)) for k in range(1, 16)]

    z_in = pltpu.make_async_copy(z_hbm, z_ref, in_sem.at[0])
    x_in = pltpu.make_async_copy(x_hbm, x_ref, in_sem.at[1])
    z_in.start()
    x_in.start()

    barrier = pltpu.get_barrier_semaphore()
    for dev in [partner] + plane_peers + z_peers:
        pl.semaphore_signal(barrier, inc=1, device_id=dev, device_id_type=MESH)

    def place(t):
        h = lax.rem(1 - zh + t // 16, 2)
        return lax.rem(t // 4, 4), h, lax.rem(t, 4)

    def tok_cols(t, side):
        y, h, x = place(t)
        src = pl.multiple_of((2 * ((y * 2 + h) * 4 + x) + side) * 128, 128)
        dst = pl.multiple_of((h * 4 + x) * 128, 128)
        return y, src, dst

    def local_tok(t):
        y, src, dst = tok_cols(t, core)
        return pltpu.make_async_copy(
            tokens.at[:, pl.ds(src, 128)], tok.at[y, 0, :, pl.ds(dst, 128)], tok_local.at[t]
        )

    def remote_tok(t):
        y, src, dst = tok_cols(t, 1 - core)
        return pltpu.make_async_remote_copy(
            src_ref=tokens.at[:, pl.ds(src, 128)],
            dst_ref=tok.at[y, 1, :, pl.ds(dst, 128)],
            send_sem=tok_send.at[t],
            recv_sem=tok_recv.at[t],
            device_id=partner,
            device_id_type=MESH,
        )

    cot_local = pltpu.make_async_copy(cot_hbm, cot.at[0], in_sem.at[2])
    cot_local.start()

    @pl.loop(0, 32)
    def _(t):
        local_tok(t).start()

    z_in.wait()
    x_in.wait()
    blended = (1.0 - beta_first) * z_ref[...] + beta_first * x_ref[...]
    wts[yc, zh, xc] = blended.astype(BF16)

    pl.semaphore_wait(barrier, 23)

    sends = []
    counter = [0]

    def message(src, dst, dev):
        m = counter[0]
        counter[0] += 1
        copy = pltpu.make_async_remote_copy(
            src_ref=src, dst_ref=dst, send_sem=send_sem.at[m], recv_sem=recv_sem.at[m],
            device_id=dev, device_id_type=MESH,
        )
        copy.start()
        sends.append(copy)
        return m

    def arrived(m, dst):
        pltpu.make_async_remote_copy(
            src_ref=dst, dst_ref=dst, send_sem=send_sem.at[m], recv_sem=recv_sem.at[m],
            device_id=partner, device_id_type=MESH,
        ).wait_recv()

    first = (xc, yc)
    second = (yc, xc)
    first_side = (x_side, y_side)
    second_side = (y_side, x_side)

    def block(p, f, s, h, r0, rows):
        y, x = (s, f) if p == 0 else (f, s)
        return wts.at[y, h, x, pl.ds(r0, rows), :]

    half_of = (zh, 1 - zh)
    ag = {}

    def spread(st, p, item):
        h = half_of[st]
        blk = block(p, mod4(first[p] + item), second[p], h, 64 * p, 64)
        for d in (0, 1):
            ag[st, p, 2, item, d] = message(blk, blk, second_side[p][d])

    def ag0(st):
        h = half_of[st]
        for p in (0, 1):
            own = block(p, first[p], second[p], h, 64 * p, 64)
            for d in (0, 1):
                ag[st, p, 0, d] = message(own, own, first_side[p][d])
        for p in (0, 1):
            spread(st, p, 0)

    def ag1(st):
        h = half_of[st]
        for p in (0, 1):
            f, s, r0 = first[p], second[p], 64 * p
            for d in (0, 1):
                src_f = mod4(f - 1 + 2 * d)
                arrived(ag[st, p, 0, d], block(p, src_f, s, h, r0, 64))
                part = block(p, src_f, s, h, r0 + 32 * d, 32)
                ag[st, p, 1, d] = message(part, part, first_side[p][d])
                spread(st, p, -1 + 2 * d)

    def ag2(st):
        h = half_of[st]
        for p in (0, 1):
            f, s, r0 = first[p], second[p], 64 * p
            for d in (0, 1):
                arrived(ag[st, p, 1, d], block(p, mod4(f + 2), s, h, r0 + 32 * d, 32))
            spread(st, p, 2)

    def ag3(st, items):
        h = half_of[st]
        for item in items:
            for p in (0, 1):
                f, s, r0 = first[p], second[p], 64 * p
                for d in (0, 1):
                    src_s = mod4(s - 1 + 2 * d)
                    arrived(ag[st, p, 2, item, d], block(p, mod4(f + item), src_s, h, r0, 64))
                    part = block(p, mod4(f + item), src_s, h, r0 + 32 * d, 32)
                    ag[st, p, 3, item, d] = message(part, part, second_side[p][d])

    def ag4(st):
        h = half_of[st]
        for item in (0, -1, 1, 2):
            for p in (0, 1):
                f, s, r0 = first[p], second[p], 64 * p
                for d in (0, 1):
                    arrived(ag[st, p, 3, item, d], block(p, mod4(f + item), mod4(s + 2), h, r0 + 32 * d, 32))

    zc = {}

    def c_row(z):
        return pl.multiple_of(lax.rem(z, 4) * C_ROWS, 16)

    def zc1(c):
        dest = z_plus(4)
        for d in (0, 1):
            half = gt.at[pl.ds(2 * c, 2), dest // 4, pl.ds(2 * d, 2), pl.ds(c_row(dest), C_ROWS), :]
            zc[1, d, c] = message(half, zc_half.at[d, c], z_side[d])

    def zc_step(s, c):
        for d in (0, 1):
            dest = z_plus((5 - s) * (1 - 2 * d))
            h, row = dest // 4, c_row(dest)
            if s == 2:
                arrived(zc[1, d, c], zc_half.at[d, c])

                @pl.loop(0, 4)
                def _(i):
                    y, x = i // 2, lax.rem(i, 2)
                    mine = gt[2 * c + y, h, 2 * d + x, pl.ds(row, C_ROWS), :].astype(F32)
                    got = zc_half[d, c, y, x].astype(F32)
                    zc_stage[0, d, c, y, 2 * d + x] = (mine + got).astype(BF16)
                    other = 2 * (1 - d) + x
                    zc_stage[0, d, c, y, other] = gt[2 * c + y, h, other, pl.ds(row, C_ROWS), :]
            else:
                arrived(zc[s - 1, d, c], zc_recv.at[s - 3, d, c])

                @pl.loop(0, 8)
                def _(i):
                    y, x = i // 4, lax.rem(i, 4)
                    mine = gt[2 * c + y, h, x, pl.ds(row, C_ROWS), :].astype(F32)
                    got = zc_recv[s - 3, d, c, y, x].astype(F32)
                    zc_stage[s - 2, d, c, y, x] = (mine + got).astype(BF16)

            zc[s, d, c] = message(zc_stage.at[s - 2, d, c], zc_recv.at[s - 2, d, c], z_side[d])

    def zc_final(c):
        for d in (0, 1):
            arrived(zc[4, d, c], zc_recv.at[2, d, c])
        row = c_row(z_now)

        @pl.loop(0, 8)
        def _(i):
            y, x = i // 4, lax.rem(i, 4)
            total = (
                gt[2 * c + y, zh, x, pl.ds(row, C_ROWS), :].astype(F32)
                + zc_recv[2, 0, c, y, x].astype(F32)
                + zc_recv[2, 1, c, y, x].astype(F32)
            )
            c_f[2 * c + y, x] = total
            c_b[2 * c + y, x] = total.astype(BF16)

    def c_send():
        out = []
        for k in range(1, 16):
            i = plane_plus(k)
            out.append(message(c_b.at[i // 4, lax.rem(i, 4)], c_recv.at[k - 1], plane_peers[k - 1]))
        return out

    def c_end(msgs):
        total = c_f[yc, xc]
        for k in range(15):
            arrived(msgs[k], c_recv.at[k])
            total = total + c_recv[k].astype(F32)
        gfull[pl.ds(c_row(z_now), C_ROWS), :] = total

    def nxt(c, d):
        return mod4(c + 1 - 2 * d)

    class Plane:
        def __init__(self, pick, load, bufs):
            self.pick, self.load, self.bufs, self.m = pick, load, bufs, {}

        def start(self, p, which):
            rel, dirc = self.bufs[0], self.bufs[1]
            for d in (0, 1):
                if which == 0:
                    src, dst = self.pick(p, mod4(first[p] + 2), d), rel.at[p, d]
                else:
                    src, dst = self.pick(p, nxt(first[p], d), 1 - d), dirc.at[p, d]
                self.m[p, which, d] = message(src, dst, first_side[p][d])

        def mid(self, p):
            rel, _, summed, stage = self.bufs[:4]
            for d in (0, 1):
                arrived(self.m[p, 0, d], rel.at[p, d])

                @pl.loop(0, 4)
                def _(i):
                    stage[p, d, i] = (self.load(p, nxt(first[p], d), d, i) + rel[p, d, i].astype(F32)).astype(BF16)

                self.m[p, 2, d] = message(stage.at[p, d], summed.at[p, d], first_side[p][d])

        def turn(self, p):
            _, dirc, summed, _, gf, gb, rel2, dir2 = self.bufs[:8]
            for d in (0, 1):
                arrived(self.m[p, 1, d], dirc.at[p, d])
                arrived(self.m[p, 2, d], summed.at[p, d])
            for h in (0, 1):
                @pl.loop(0, 4)
                def _(i):
                    total = (
                        self.load(p, first[p], h, i)
                        + dirc[p, 1 - h, i].astype(F32)
                        + summed[p, h, i].astype(F32)
                    )
                    gf[p, i, h] = total
                    gb[p, i, h] = total.astype(BF16)
            s = second[p]
            for d in (0, 1):
                self.m[p, 3, d] = message(gb.at[p, mod4(s + 2), d], rel2.at[p, d], second_side[p][d])
            for d in (0, 1):
                self.m[p, 4, d] = message(gb.at[p, nxt(s, d), 1 - d], dir2.at[p, d], second_side[p][d])

        def mid2(self, p):
            gf, _, rel2, _, summed2, stage2_ = self.bufs[4:]
            for d in (0, 1):
                arrived(self.m[p, 3, d], rel2.at[p, d])
                stage2_[p, d] = (gf[p, nxt(second[p], d), d] + rel2[p, d].astype(F32)).astype(BF16)
                self.m[p, 5, d] = message(stage2_.at[p, d], summed2.at[p, d], second_side[p][d])

        def end(self, p):
            gf, _, _, dir2, summed2, _ = self.bufs[4:]
            for d in (0, 1):
                arrived(self.m[p, 4, d], dir2.at[p, d])
                arrived(self.m[p, 5, d], summed2.at[p, d])
            return [
                gf[p, second[p], h] + dir2[p, 1 - h].astype(F32) + summed2[p, h].astype(F32)
                for h in (0, 1)
            ]

    def ab_pick(p, f, h):
        rows = pl.ds(AB + R * p, R)
        return gt.at[:, h, f, rows, :] if p == 0 else gt.at[f, h, :, rows, :]

    def ab_load(p, f, h, i):
        rows = pl.ds(AB + R * p, R)
        return (gt[i, h, f, rows, :] if p == 0 else gt[f, h, i, rows, :]).astype(F32)

    ab = Plane(ab_pick, ab_load, (relay1, direct1, summed1, stage1, g1f, g1b, relay2, direct2, summed2, stage2))

    def grad(j0, j1):
        @pl.loop(j0, j1)
        def _(j):
            for t in (2 * j, 2 * j + 1):
                local_tok(t).wait()
                remote_tok(t).wait_recv()
            y, h, x = place(2 * j)
            col = pl.multiple_of(h * 512 + x * 128, 256)
            rhs = tok[y, :, :, pl.ds(col, 256)].reshape(1024, 256)
            for q in (0, 1):
                rows = slice(256 * q, 256 * (q + 1))
                out = jnp.dot(cot_t[rows, :], rhs, preferred_element_type=F32).astype(BF16)
                gt[y, h, x, rows, :] = out[:, :128]
                gt[y, h, x + 1, rows, :] = out[:, 128:]

    def values(st, y, m):
        h = half_of[st]
        lhs = tok[y, m, :, pl.ds(pl.multiple_of(h * 512, 512), 512)]
        out = jnp.dot(lhs, wts[y, h].reshape(512, 512), preferred_element_type=F32)
        acc[m] = out if (st, y) == (0, 0) else acc[m] + out

    def z_send():
        out = []
        for k in range(1, 8):
            dest = z_plus(k)
            part = zstage.at[dest // 4, pl.ds(pl.multiple_of(lax.rem(dest, 4) * Q, 16), Q), :]
            out.append(message(part, zrecv.at[k - 1], z_peers[k - 1]))
        return out

    def z_end(msgs):
        total = plane[zh, pl.ds(pl.multiple_of(zl * Q, 16), Q), :]
        for k in range(7):
            arrived(msgs[k], zrecv.at[k])
            total = total + zrecv[k].astype(F32)
        gfull[pl.ds(pl.multiple_of(AB + zl * Q, 16), Q), :] = total

    def share(base, n):
        rows = gfull.at[pl.ds(pl.multiple_of(base + zl * n, 16), n), :]
        return [message(rows, rows, (lax.rem(zl + k, 4), index)) for k in range(1, 4)]

    def shared(base, n, msgs):
        for k in range(1, 4):
            row = pl.multiple_of(base + lax.rem(zl + 4 - k, 4) * n, 16)
            arrived(msgs[k - 1], gfull.at[pl.ds(row, n), :])

    def ab_start(which):
        for p in (0, 1):
            ab.start(p, which)

    def ab_all(step):
        for p in (0, 1):
            step(p)

    def ab_end():
        for p in (0, 1):
            for h, total in enumerate(ab.end(p)):
                plane[h, R * p:R * (p + 1), :] = total
                zstage[h, R * p:R * (p + 1), :] = total.astype(BF16)

    cot_msg = message(cot_hbm, cot.at[1], partner)
    ag0(0)

    @pl.loop(0, 32)
    def _(t):
        remote_tok(t).start()

    own = wts.at[yc, zh, xc]
    mirror_msg = message(own, own, mirror)
    cot_local.wait()
    arrived(cot_msg, cot.at[1])
    for k in (0, 1):
        cot_t[:, 512 * k:512 * (k + 1)] = cot[k].T
    grad(0, 2)
    grad(2, 4)
    zc1(0)
    grad(4, 6)
    grad(6, 8)
    zc1(1)
    ag1(0)
    grad(8, 10)
    grad(10, 12)
    grad(12, 14)
    grad(14, 16)
    ab_start(0)
    zc_step(2, 0)
    ag2(0)
    ag3(0, (0,))
    ab_start(1)
    arrived(mirror_msg, wts.at[yc, 1 - zh, xc])
    ag0(1)
    zc_step(2, 1)
    ag3(0, (-1, 1))
    zc_step(3, 0)
    zc_step(3, 1)
    ag3(0, (2,))
    ab_all(ab.mid)
    ag1(1)
    ag3(1, (0,))
    ag4(0)
    values(0, 0, 0)
    values(0, 0, 1)
    values(0, 1, 0)
    values(0, 1, 1)
    values(0, 2, 0)
    values(0, 2, 1)
    zc_step(4, 0)
    values(0, 3, 0)
    values(0, 3, 1)
    zc_step(4, 1)
    ag2(1)
    ab_all(ab.turn)
    ag3(1, (-1, 1))
    ag3(1, (2,))
    ab_all(ab.mid2)
    zc_final(0)
    zc_final(1)
    ab_end()
    z_msgs = z_send()
    c_msgs = c_send()
    ag4(1)
    values(1, 0, 1)
    values(1, 1, 1)
    values(1, 2, 1)
    values(1, 3, 1)
    values(1, 0, 0)
    values(1, 1, 0)
    values(1, 2, 0)
    values(1, 3, 0)
    z_end(z_msgs)
    ab_share = share(AB, Q)
    vmsg = message(acc.at[1], vrecv, partner)
    c_end(c_msgs)
    c_share = share(0, C_ROWS)
    arrived(vmsg, vrecv)
    values_out[...] = ((acc[0] + vrecv[...]) * NORM).astype(BF16)
    shared(0, C_ROWS, c_share)
    shared(AB, Q, ab_share)
    grad_out[...] = gfull[...]

    for copy in sends:
        copy.wait_send()

    @pl.loop(0, 32)
    def _(t):
        remote_tok(t).wait_send()

    assert counter[0] <= N_MSG


def finish(values_ref, grad_ref, z_ref, x_ref, s_ref, values_out, z_out, x_out, s_out):
    values_out[...] = values_ref[...]
    gradient = grad_ref[...].T * NORM
    z_in = z_ref[...]
    x_in = x_ref[...]
    mixed = (1.0 - beta_first) * z_in + beta_first * x_in
    second_next = beta_second * s_ref[...] + (1.0 - beta_second) * gradient * gradient
    scaled = gradient / (jnp.sqrt(second_next / bias_fix) + epsilon)
    z_next = z_in - learn_rate * (scaled + weight_decay * mixed)
    s_out[...] = second_next
    z_out[...] = z_next
    x_out[...] = (1.0 - mixing) * x_in + mixing * z_next


def local(tokens, cotangent, z_weights, x_weights, second_moment):
    vm = pl.BlockSpec(memory_space=pltpu.VMEM)
    hbm = pl.BlockSpec(memory_space=pl.ANY)
    shard = jax.ShapeDtypeStruct((128, HV), F32)
    vals = jax.ShapeDtypeStruct((TOK, HV), BF16)
    dma = pltpu.SemaphoreType.DMA

    def plane_bufs(r):
        return (
            [pltpu.VMEM((2, 2, 4, r, 128), BF16)] * 4
            + [pltpu.VMEM((2, 4, 2, r, 128), F32), pltpu.VMEM((2, 4, 2, r, 128), BF16)]
            + [pltpu.VMEM((2, 2, r, 128), BF16)] * 4
        )

    values, gradient = pl.pallas_call(
        kernel,
        out_shape=(vals, jax.ShapeDtypeStruct((HV, 128), F32)),
        in_specs=[hbm, hbm, hbm, hbm],
        out_specs=(vm, vm),
        scratch_shapes=[
            pltpu.VMEM((128, HV), F32),
            pltpu.VMEM((128, HV), F32),
            pltpu.VMEM((4, 2, 512, 1024), BF16),
            pltpu.VMEM((2, 512, 512), BF16),
            pltpu.VMEM((512, 1024), BF16),
            pltpu.VMEM((4, 2, 4, 128, 512), BF16),
            pltpu.VMEM((4, 2, 4, 512, 128), BF16),
        ] + plane_bufs(R) + [
            pltpu.VMEM((4, 4, C_ROWS, 128), F32),
            pltpu.VMEM((4, 4, C_ROWS, 128), BF16),
            pltpu.VMEM((15, C_ROWS, 128), BF16),
            pltpu.VMEM((2, 2, 2, 2, C_ROWS, 128), BF16),
            pltpu.VMEM((3, 2, 2, 2, 4, C_ROWS, 128), BF16),
            pltpu.VMEM((3, 2, 2, 2, 4, C_ROWS, 128), BF16),
            pltpu.VMEM((2, 2 * R, 128), F32),
            pltpu.VMEM((2, 2 * R, 128), BF16),
            pltpu.VMEM((7, Q, 128), BF16),
            pltpu.VMEM((512, 128), F32),
            pltpu.VMEM((2, 512, 512), F32),
            pltpu.VMEM((512, 512), F32),
            dma((N_MSG,)),
            dma((N_MSG,)),
            dma((32,)),
            dma((32,)),
            dma((32,)),
            dma((3,)),
        ],
        compiler_params=pltpu.CompilerParams(
            collective_id=0, has_side_effects=True, vmem_limit_bytes=48 * 1024 * 1024
        ),
    )(tokens, *[pltpu.with_memory_space_constraint(a, pltpu.HBM) for a in (cotangent, z_weights, x_weights)])
    return pl.pallas_call(
        finish,
        out_shape=(vals, shard, shard, shard),
        in_specs=[vm] * 5,
        out_specs=(vm,) * 4,
        compiler_params=pltpu.CompilerParams(vmem_limit_bytes=12 * 1024 * 1024),
    )(values, gradient, z_weights, x_weights, second_moment)


def solution(mesh):
    return jax.shard_map(
        local,
        mesh=mesh,
        in_specs=(
            P(("replica", "fsdp"), None),
            P(("replica", "fsdp"), None),
            P("fsdp", None),
            P("fsdp", None),
            P("fsdp", None),
        ),
        out_specs=(P(("replica", "fsdp"), None), P("fsdp", None), P("fsdp", None), P("fsdp", None)),
        check_vma=False,
    )
```

```python
import math

import jax
import jax.numpy as jnp
from jax import lax
from jax.experimental import pallas as pl
from jax.experimental.pallas import tpu as pltpu
from jax.sharding import PartitionSpec as P

beta_first = 0.9
beta_second = 0.95
learn_rate = 0.25
weight_decay = 0.1
step_count = 8.0
epsilon = 1e-08
bias_fix = 1.0 - 0.95**8
mixing = 1.0 / (step_count + 1.0)

D = 8192
HV = 512
TOK = 512
NORM = 1.0 / math.sqrt(D)
F32 = jnp.float32
BF16 = jnp.bfloat16
MESH = pl.DeviceIdType.MESH
N_MSG = 192
C_ROWS = 80
CHUNKS = (48, 32)
AB = 4 * C_ROWS
R = (HV - AB) // 2
Q = R // 2


def kernel(
    tokens, cot_hbm, z_hbm, x_hbm,
    values_out, grad_out,
    z_ref, x_ref, tok, cot, cot_t, wts, gt,
    relay1, direct1, summed1, stage1, g1f, g1b, relay2, direct2, summed2, stage2,
    plane, zstage, zrecv, gfull, acc, vrecv,
    send_sem, recv_sem, tok_local, tok_send, tok_recv, in_sem,
    *chunk_refs,
):
    zl = lax.axis_index("replica")
    index = lax.axis_index("fsdp")
    core = lax.rem(index, 2)
    xc = lax.rem(index // 2, 4)
    zh = lax.rem(index // 8, 2)
    yc = index // 16

    def fsdp_of(y, h, x):
        return ((y * 2 + h) * 4 + x) * 2 + core

    def mod4(v):
        return lax.rem(v + 8, 4)

    partner = (zl, index + 1 - 2 * core)
    x_side = [(zl, fsdp_of(yc, zh, mod4(xc + d))) for d in (1, -1)]
    y_side = [(zl, fsdp_of(mod4(yc + d), zh, xc)) for d in (1, -1)]
    z_now = zh * 4 + zl

    def z_plus(k):
        return lax.rem(z_now + k + 8, 8)

    def z_dev(z):
        return (lax.rem(z, 4), fsdp_of(yc, z // 4, xc))

    z_peers = [z_dev(z_plus(k)) for k in range(1, 8)]
    z_side = [z_dev(z_plus(1)), z_dev(z_plus(-1))]
    at_cut = lax.rem(zl, 3) == 0
    outward = 2 * (zl // 2) - 1
    outer, inner = z_dev(z_plus(outward)), z_dev(z_plus(-outward))

    def plane_plus(k):
        return lax.rem(yc * 4 + xc + k, 16)

    def plane_dev(i):
        return (zl, fsdp_of(i // 4, zh, lax.rem(i, 4)))

    plane_peers = [plane_dev(plane_plus(k)) for k in range(1, 16)]

    z_in = pltpu.make_async_copy(z_hbm, z_ref, in_sem.at[0])
    x_in = pltpu.make_async_copy(x_hbm, x_ref, in_sem.at[1])
    z_in.start()
    x_in.start()

    barrier = pltpu.get_barrier_semaphore()
    for dev in [partner] + plane_peers + z_peers:
        pl.semaphore_signal(barrier, inc=1, device_id=dev, device_id_type=MESH)

    def place(t):
        h = lax.rem(1 - zh + t // 16, 2)
        return lax.rem(t // 4, 4), h, lax.rem(t, 4)

    def tok_cols(t, side):
        y, h, x = place(t)
        src = pl.multiple_of((2 * ((y * 2 + h) * 4 + x) + side) * 128, 128)
        dst = pl.multiple_of((h * 4 + x) * 128, 128)
        return y, src, dst

    def local_tok(t):
        y, src, dst = tok_cols(t, core)
        return pltpu.make_async_copy(
            tokens.at[:, pl.ds(src, 128)], tok.at[y, 0, :, pl.ds(dst, 128)], tok_local.at[t]
        )

    def remote_tok(t):
        y, src, dst = tok_cols(t, 1 - core)
        return pltpu.make_async_remote_copy(
            src_ref=tokens.at[:, pl.ds(src, 128)],
            dst_ref=tok.at[y, 1, :, pl.ds(dst, 128)],
            send_sem=tok_send.at[t],
            recv_sem=tok_recv.at[t],
            device_id=partner,
            device_id_type=MESH,
        )

    cot_local = pltpu.make_async_copy(cot_hbm, cot.at[0], in_sem.at[2])
    cot_local.start()

    @pl.loop(0, 32)
    def _(t):
        local_tok(t).start()

    z_in.wait()
    x_in.wait()
    blended = (1.0 - beta_first) * z_ref[...] + beta_first * x_ref[...]
    wts[yc, zh, xc] = blended.astype(BF16)

    pl.semaphore_wait(barrier, 23)

    sends = []
    counter = [0]

    def message(src, dst, dev):
        m = counter[0]
        counter[0] += 1
        copy = pltpu.make_async_remote_copy(
            src_ref=src, dst_ref=dst, send_sem=send_sem.at[m], recv_sem=recv_sem.at[m],
            device_id=dev, device_id_type=MESH,
        )
        copy.start()
        sends.append(copy)
        return m

    def arrived(m, dst):
        pltpu.make_async_remote_copy(
            src_ref=dst, dst_ref=dst, send_sem=send_sem.at[m], recv_sem=recv_sem.at[m],
            device_id=partner, device_id_type=MESH,
        ).wait_recv()

    first = (xc, yc)
    second = (yc, xc)
    first_side = (x_side, y_side)
    second_side = (y_side, x_side)

    def block(p, f, s, h, r0, rows):
        y, x = (s, f) if p == 0 else (f, s)
        return wts.at[y, h, x, pl.ds(r0, rows), :]

    half_of = (zh, 1 - zh)
    ag = {}

    def spread(st, p, item):
        h = half_of[st]
        blk = block(p, mod4(first[p] + item), second[p], h, 64 * p, 64)
        for d in (0, 1):
            ag[st, p, 2, item, d] = message(blk, blk, second_side[p][d])

    def ag0(st):
        h = half_of[st]
        for p in (0, 1):
            own = block(p, first[p], second[p], h, 64 * p, 64)
            for d in (0, 1):
                ag[st, p, 0, d] = message(own, own, first_side[p][d])
    def spread_own(st):
        for p in (0, 1):
            spread(st, p, 0)

    def spread_next(st):
        for p in (0, 1):
            for item in (-1, 1):
                spread(st, p, item)

    def ag1(st):
        h = half_of[st]
        for p in (0, 1):
            f, s, r0 = first[p], second[p], 64 * p
            for d in (0, 1):
                src_f = mod4(f - 1 + 2 * d)
                arrived(ag[st, p, 0, d], block(p, src_f, s, h, r0, 64))
                part = block(p, src_f, s, h, r0 + 32 * d, 32)
                ag[st, p, 1, d] = message(part, part, first_side[p][d])

    def ag2(st):
        h = half_of[st]
        for p in (0, 1):
            f, s, r0 = first[p], second[p], 64 * p
            for d in (0, 1):
                arrived(ag[st, p, 1, d], block(p, mod4(f + 2), s, h, r0 + 32 * d, 32))
            spread(st, p, 2)

    def ag3(st, items):
        h = half_of[st]
        for item in items:
            for p in (0, 1):
                f, s, r0 = first[p], second[p], 64 * p
                for d in (0, 1):
                    src_s = mod4(s - 1 + 2 * d)
                    arrived(ag[st, p, 2, item, d], block(p, mod4(f + item), src_s, h, r0, 64))
                    part = block(p, mod4(f + item), src_s, h, r0 + 32 * d, 32)
                    ag[st, p, 3, item, d] = message(part, part, second_side[p][d])

    def ag4(st):
        h = half_of[st]
        for item in (0, -1, 1, 2):
            for p in (0, 1):
                f, s, r0 = first[p], second[p], 64 * p
                for d in (0, 1):
                    arrived(ag[st, p, 3, item, d], block(p, mod4(f + item), mod4(s + 2), h, r0 + 32 * d, 32))

    zc = {}

    starts = [sum(CHUNKS[:c]) for c in range(len(CHUNKS))]
    chunk = [chunk_refs[6 * c:6 * c + 6] for c in range(len(CHUNKS))]

    def c_row(z, c):
        return pl.ds(pl.multiple_of(lax.rem(z, 4) * C_ROWS + starts[c], 16), CHUNKS[c])

    def zc1(c):
        dest = z_plus(4)
        for d in (0, 1):
            half = gt.at[:, dest // 4, pl.ds(2 * d, 2), c_row(dest, c), :]
            zc[1, d, c] = message(half, chunk[c][0].at[d], z_side[d])

    def zc_step(s, c):
        zc_half, zc_recv, zc_stage = chunk[c][:3]
        for d in (0, 1):
            dest = z_plus((5 - s) * (1 - 2 * d))
            h, row = dest // 4, c_row(dest, c)
            if s == 2:
                arrived(zc[1, d, c], zc_half.at[d])

                @pl.loop(0, 8)
                def _(i):
                    y, x = i // 2, lax.rem(i, 2)
                    mine = gt[y, h, 2 * d + x, row, :].astype(F32)
                    got = zc_half[d, y, x].astype(F32)
                    zc_stage[0, d, y, 2 * d + x] = (mine + got).astype(BF16)
                    other = 2 * (1 - d) + x
                    zc_stage[0, d, y, other] = gt[y, h, other, row, :]
            else:
                arrived(zc[s - 1, d, c], zc_recv.at[s - 3, d])

                @pl.loop(0, 16)
                def _(i):
                    y, x = i // 4, lax.rem(i, 4)
                    mine = gt[y, h, x, row, :].astype(F32)
                    got = zc_recv[s - 3, d, y, x].astype(F32)
                    zc_stage[s - 2, d, y, x] = (mine + got).astype(BF16)

            zc[s, d, c] = message(zc_stage.at[s - 2, d], zc_recv.at[s - 2, d], z_side[d])

    def zc_final(c):
        _, zc_recv, _, c_f, c_b, _ = chunk[c]
        for d in (0, 1):
            arrived(zc[4, d, c], zc_recv.at[2, d])
        row = c_row(z_now, c)

        @pl.loop(0, 16)
        def _(i):
            y, x = i // 4, lax.rem(i, 4)
            total = (
                gt[y, zh, x, row, :].astype(F32)
                + zc_recv[2, 0, y, x].astype(F32)
                + zc_recv[2, 1, y, x].astype(F32)
            )
            c_f[y, x] = total
            c_b[y, x] = total.astype(BF16)

    c_msgs = {}
    shares = {}

    def c_send(c):
        c_b, c_recv = chunk[c][4:]
        for k in range(1, 16):
            i = plane_plus(k)
            c_msgs[c, k] = message(c_b.at[i // 4, lax.rem(i, 4)], c_recv.at[k - 1], plane_peers[k - 1])

    def c_end(c):
        c_f, _, c_recv = chunk[c][3:]
        total = c_f[yc, xc]
        for k in range(1, 16):
            arrived(c_msgs[c, k], c_recv.at[k - 1])
            total = total + c_recv[k - 1].astype(F32)
        gfull[c_row(z_now, c), :] = total
        share(c)

    def nxt(c, d):
        return mod4(c + 1 - 2 * d)

    class Plane:
        def __init__(self, pick, load, bufs):
            self.pick, self.load, self.bufs, self.m = pick, load, bufs, {}

        def start(self, p, which):
            rel, dirc = self.bufs[0], self.bufs[1]
            for d in (0, 1):
                if which == 0:
                    src, dst = self.pick(p, mod4(first[p] + 2), d), rel.at[p, d]
                else:
                    src, dst = self.pick(p, nxt(first[p], d), 1 - d), dirc.at[p, d]
                self.m[p, which, d] = message(src, dst, first_side[p][d])

        def mid(self, p):
            rel, _, summed, stage = self.bufs[:4]
            for d in (0, 1):
                arrived(self.m[p, 0, d], rel.at[p, d])

                @pl.loop(0, 4)
                def _(i):
                    stage[p, d, i] = (self.load(p, nxt(first[p], d), d, i) + rel[p, d, i].astype(F32)).astype(BF16)

                self.m[p, 2, d] = message(stage.at[p, d], summed.at[p, d], first_side[p][d])

        def turn(self, p):
            _, dirc, summed, _, gf, gb, rel2 = self.bufs[:7]
            for d in (0, 1):
                arrived(self.m[p, 1, d], dirc.at[p, d])
                arrived(self.m[p, 2, d], summed.at[p, d])
            for h in (0, 1):
                @pl.loop(0, 4)
                def _(i):
                    total = (
                        self.load(p, first[p], h, i)
                        + dirc[p, 1 - h, i].astype(F32)
                        + summed[p, h, i].astype(F32)
                    )
                    gf[p, i, h] = total
                    gb[p, i, h] = total.astype(BF16)
            for d in (0, 1):
                src = gb.at[p, mod4(second[p] + 2), d]
                self.m[p, 3, d] = message(src, rel2.at[p, d], second_side[p][d])

        def turn2(self, p):
            gb, _, dir2 = self.bufs[5:8]
            for d in (0, 1):
                src = gb.at[p, nxt(second[p], d), 1 - d]
                self.m[p, 4, d] = message(src, dir2.at[p, d], second_side[p][d])

        def mid2(self, p):
            gf, _, rel2, _, summed2, stage2_ = self.bufs[4:]
            for d in (0, 1):
                arrived(self.m[p, 3, d], rel2.at[p, d])
                stage2_[p, d] = (gf[p, nxt(second[p], d), d] + rel2[p, d].astype(F32)).astype(BF16)
                self.m[p, 5, d] = message(stage2_.at[p, d], summed2.at[p, d], second_side[p][d])

        def end(self, p):
            gf, _, _, dir2, summed2, _ = self.bufs[4:]
            for d in (0, 1):
                arrived(self.m[p, 4, d], dir2.at[p, d])
                arrived(self.m[p, 5, d], summed2.at[p, d])
            return [
                gf[p, second[p], h] + dir2[p, 1 - h].astype(F32) + summed2[p, h].astype(F32)
                for h in (0, 1)
            ]

    def ab_pick(p, f, h):
        rows = pl.ds(AB + R * p, R)
        return gt.at[:, h, f, rows, :] if p == 0 else gt.at[f, h, :, rows, :]

    def ab_load(p, f, h, i):
        rows = pl.ds(AB + R * p, R)
        return (gt[i, h, f, rows, :] if p == 0 else gt[f, h, i, rows, :]).astype(F32)

    ab = Plane(ab_pick, ab_load, (relay1, direct1, summed1, stage1, g1f, g1b, relay2, direct2, summed2, stage2))

    def grad(j0, j1):
        @pl.loop(j0, j1)
        def _(j):
            for t in (2 * j, 2 * j + 1):
                local_tok(t).wait()
                remote_tok(t).wait_recv()
            y, h, x = place(2 * j)
            col = pl.multiple_of(h * 512 + x * 128, 256)
            rhs = tok[y, :, :, pl.ds(col, 256)].reshape(1024, 256)
            for q in (0, 1):
                rows = slice(256 * q, 256 * (q + 1))
                out = jnp.dot(cot_t[rows, :], rhs, preferred_element_type=F32).astype(BF16)
                gt[y, h, x, rows, :] = out[:, :128]
                gt[y, h, x + 1, rows, :] = out[:, 128:]

    def values(st, y, m):
        h = half_of[st]
        lhs = tok[y, m, :, pl.ds(pl.multiple_of(h * 512, 512), 512)]
        out = jnp.dot(lhs, wts[y, h].reshape(512, 512), preferred_element_type=F32)
        acc[m] = out if (st, y) == (0, 0) else acc[m] + out

    def values2(st, y, m):
        h = half_of[st]
        cols = pl.ds(pl.multiple_of(h * 512, 512), 512)
        total = acc[m]
        for k in (0, 1):
            rhs = wts[y + k, h].reshape(512, 512)
            total = total + jnp.dot(tok[y + k, m, :, cols], rhs, preferred_element_type=F32)
        acc[m] = total

    def z_send():
        out = []
        for k in range(1, 8):
            dest = z_plus(k)
            part = zstage.at[dest // 4, pl.ds(pl.multiple_of(lax.rem(dest, 4) * Q, 16), Q), :]
            out.append(message(part, zrecv.at[k - 1], z_peers[k - 1]))
        return out

    def z_end(msgs):
        total = plane[zh, pl.ds(pl.multiple_of(zl * Q, 16), Q), :]
        for k in range(7):
            arrived(msgs[k], zrecv.at[k])
            total = total + zrecv[k].astype(F32)
        gfull[rows_of(zl, "ab"), :] = total
        share("ab")

    def rows_of(z, part):
        if part == "ab":
            return pl.ds(pl.multiple_of(AB + lax.rem(z, 4) * Q, 16), Q)
        return c_row(z, part)

    def share(part):
        rows = gfull.at[rows_of(zl, part), :]
        for k in range(1, 4):
            shares[part, k] = message(rows, rows, (lax.rem(zl + k, 4), index))

    def shared(part):
        for k in range(1, 4):
            arrived(shares[part, k], gfull.at[rows_of(zl + 4 - k, part), :])

    def cut_copy(n, src, dev):
        m = N_MSG - 2 + n
        return pltpu.make_async_remote_copy(
            src_ref=src, dst_ref=src, send_sem=send_sem.at[m], recv_sem=recv_sem.at[m],
            device_id=dev, device_id_type=MESH,
        )

    own_block = wts.at[yc, zh, xc]
    other_block = wts.at[yc, 1 - zh, xc]

    def cut_send():
        @pl.when(at_cut)
        def _():
            cut_copy(0, own_block, outer).start()

    def cut_forward():
        @pl.when(at_cut)
        def _():
            cut_copy(0, other_block, outer).wait_recv()
            cut_copy(1, other_block, inner).start()

    def cut_end():
        @pl.when(jnp.logical_not(at_cut))
        def _():
            cut_copy(1, other_block, outer).wait_recv()

    def ab_start(which):
        for p in (0, 1):
            ab.start(p, which)

    def ab_all(step):
        for p in (0, 1):
            step(p)

    def ab_end():
        for p in (0, 1):
            for h, total in enumerate(ab.end(p)):
                plane[h, R * p:R * (p + 1), :] = total
                zstage[h, R * p:R * (p + 1), :] = total.astype(BF16)

    def finish_sends(lo, hi):
        for copy in sends[lo:hi]:
            copy.wait_send()

    def finish_early():
        finish_sends(0, early)

        @pl.when(at_cut)
        def _():
            cut_copy(0, own_block, outer).wait_send()
            cut_copy(1, other_block, inner).wait_send()

        @pl.loop(0, 32)
        def _(t):
            remote_tok(t).wait_send()

    cot_msg = message(cot_hbm, cot.at[1], partner)
    ag0(0)
    cut_send()

    @pl.loop(0, 32)
    def _(t):
        remote_tok(t).start()

    cot_local.wait()
    cot_t[:, :512] = cot[0].T
    arrived(cot_msg, cot.at[1])
    cot_t[:, 512:] = cot[1].T
    grad(0, 2)
    spread_own(0)
    grad(2, 4)
    grad(4, 6)
    grad(6, 8)
    zc1(1)
    zc1(0)
    ag1(0)
    spread_next(0)
    cut_forward()
    ag3(0, (0,))
    grad(8, 10)
    grad(10, 12)
    grad(12, 14)
    grad(14, 16)
    ab_start(0)
    ab_start(1)
    ag2(0)
    zc_step(2, 1)
    ag3(0, (-1, 1))
    zc_step(2, 0)
    cut_end()
    ag0(1)
    spread_own(1)
    ag3(0, (2,))
    zc_step(3, 1)
    ab_all(ab.mid)
    zc_step(3, 0)
    ag4(0)
    values(0, 0, 0)
    ag1(1)
    spread_next(1)
    values(0, 0, 1)
    values(0, 1, 0)
    values(0, 1, 1)
    values(0, 2, 0)
    values(0, 2, 1)
    values(0, 3, 0)
    values(0, 3, 1)
    zc_step(4, 1)
    ab_all(ab.turn)
    ag2(1)
    ag3(1, (0,))
    ab_all(ab.turn2)
    zc_step(4, 0)
    ag3(1, (-1, 1))
    ab_all(ab.mid2)
    zc_final(1)
    c_send(1)
    ab_end()
    z_msgs = z_send()
    ag3(1, (2,))
    zc_final(0)
    c_send(0)
    c_end(1)
    ag4(1)
    values2(1, 0, 1)
    values2(1, 2, 1)
    z_end(z_msgs)
    vmsg = message(acc.at[1], vrecv, partner)
    values2(1, 0, 0)
    values2(1, 2, 0)
    c_end(0)
    early = counter[0] - 30
    finish_early()
    arrived(vmsg, vrecv)
    values_out[...] = ((acc[0] + vrecv[...]) * NORM).astype(BF16)
    for part in (*range(2), "ab"):
        shared(part)
    grad_out[...] = gfull[...]

    finish_sends(early, len(sends))

    assert counter[0] <= N_MSG - 2


def finish(values_ref, grad_ref, z_ref, x_ref, s_ref, values_out, z_out, x_out, s_out):
    values_out[...] = values_ref[...]
    gradient = grad_ref[...].T * NORM
    z_in = z_ref[...]
    x_in = x_ref[...]
    mixed = (1.0 - beta_first) * z_in + beta_first * x_in
    second_next = beta_second * s_ref[...] + (1.0 - beta_second) * gradient * gradient
    scaled = gradient / (jnp.sqrt(second_next / bias_fix) + epsilon)
    z_next = z_in - learn_rate * (scaled + weight_decay * mixed)
    s_out[...] = second_next
    z_out[...] = z_next
    x_out[...] = (1.0 - mixing) * x_in + mixing * z_next


def local(tokens, cotangent, z_weights, x_weights, second_moment):
    vm = pl.BlockSpec(memory_space=pltpu.VMEM)
    hbm = pl.BlockSpec(memory_space=pl.ANY)
    shard = jax.ShapeDtypeStruct((128, HV), F32)
    vals = jax.ShapeDtypeStruct((TOK, HV), BF16)
    dma = pltpu.SemaphoreType.DMA

    def plane_bufs(r):
        return (
            [pltpu.VMEM((2, 2, 4, r, 128), BF16)] * 4
            + [pltpu.VMEM((2, 4, 2, r, 128), F32), pltpu.VMEM((2, 4, 2, r, 128), BF16)]
            + [pltpu.VMEM((2, 2, r, 128), BF16)] * 4
        )

    def chunk_bufs(r):
        return [
            pltpu.VMEM((2, 4, 2, r, 128), BF16),
            pltpu.VMEM((3, 2, 4, 4, r, 128), BF16),
            pltpu.VMEM((3, 2, 4, 4, r, 128), BF16),
            pltpu.VMEM((4, 4, r, 128), F32),
            pltpu.VMEM((4, 4, r, 128), BF16),
            pltpu.VMEM((15, r, 128), BF16),
        ]

    values, gradient = pl.pallas_call(
        kernel,
        out_shape=(vals, jax.ShapeDtypeStruct((HV, 128), F32)),
        in_specs=[hbm, hbm, hbm, hbm],
        out_specs=(vm, vm),
        scratch_shapes=[
            pltpu.VMEM((128, HV), F32),
            pltpu.VMEM((128, HV), F32),
            pltpu.VMEM((4, 2, 512, 1024), BF16),
            pltpu.VMEM((2, 512, 512), BF16),
            pltpu.VMEM((512, 1024), BF16),
            pltpu.VMEM((4, 2, 4, 128, 512), BF16),
            pltpu.VMEM((4, 2, 4, 512, 128), BF16),
        ] + plane_bufs(R) + [
            pltpu.VMEM((2, 2 * R, 128), F32),
            pltpu.VMEM((2, 2 * R, 128), BF16),
            pltpu.VMEM((7, Q, 128), BF16),
            pltpu.VMEM((512, 128), F32),
            pltpu.VMEM((2, 512, 512), F32),
            pltpu.VMEM((512, 512), F32),
            dma((N_MSG,)),
            dma((N_MSG,)),
            dma((32,)),
            dma((32,)),
            dma((32,)),
            dma((3,)),
        ] + [ref for r in CHUNKS for ref in chunk_bufs(r)],
        compiler_params=pltpu.CompilerParams(
            collective_id=0, has_side_effects=True, vmem_limit_bytes=48 * 1024 * 1024
        ),
    )(tokens, *[pltpu.with_memory_space_constraint(a, pltpu.HBM) for a in (cotangent, z_weights, x_weights)])
    return pl.pallas_call(
        finish,
        out_shape=(vals, shard, shard, shard),
        in_specs=[vm] * 5,
        out_specs=(vm,) * 4,
        compiler_params=pltpu.CompilerParams(vmem_limit_bytes=12 * 1024 * 1024),
    )(values, gradient, z_weights, x_weights, second_moment)


def solution(mesh):
    return jax.shard_map(
        local,
        mesh=mesh,
        in_specs=(
            P(("replica", "fsdp"), None),
            P(("replica", "fsdp"), None),
            P("fsdp", None),
            P("fsdp", None),
            P("fsdp", None),
        ),
        out_specs=(P(("replica", "fsdp"), None), P("fsdp", None), P("fsdp", None), P("fsdp", None)),
        check_vma=False,
    )
```

```python
import math

import jax
import jax.numpy as jnp
from jax import lax
from jax.experimental import pallas as pl
from jax.experimental.pallas import tpu as pltpu
from jax.sharding import PartitionSpec as P

beta_first = 0.9
beta_second = 0.95
learn_rate = 0.25
weight_decay = 0.1
step_count = 8.0
epsilon = 1e-08
bias_fix = 1.0 - 0.95**8
mixing = 1.0 / (step_count + 1.0)

D = 8192
HV = 512
TOK = 512
NORM = 1.0 / math.sqrt(D)
F32 = jnp.float32
BF16 = jnp.bfloat16
MESH = pl.DeviceIdType.MESH
N_MSG = 192
C_ROWS = 80
CHUNKS = (48, 32)
AB = 4 * C_ROWS
R = (HV - AB) // 2
Q = R // 2


def kernel(
    tokens, cot_hbm, z_hbm, x_hbm,
    values_out, grad_out,
    z_ref, x_ref, tok, cot, cot_t, wts, gt,
    relay1, direct1, summed1, stage1, g1f, g1b, relay2, direct2, summed2, stage2,
    plane, zstage, zrecv, gfull, acc, vrecv,
    send_sem, recv_sem, tok_local, tok_send, tok_recv, in_sem,
    *chunk_refs,
):
    zl = lax.axis_index("replica")
    index = lax.axis_index("fsdp")
    core = lax.rem(index, 2)
    xc = lax.rem(index // 2, 4)
    zh = lax.rem(index // 8, 2)
    yc = index // 16

    def fsdp_of(y, h, x):
        return ((y * 2 + h) * 4 + x) * 2 + core

    def mod4(v):
        return lax.rem(v + 8, 4)

    partner = (zl, index + 1 - 2 * core)
    x_side = [(zl, fsdp_of(yc, zh, mod4(xc + d))) for d in (1, -1)]
    y_side = [(zl, fsdp_of(mod4(yc + d), zh, xc)) for d in (1, -1)]
    z_now = zh * 4 + zl

    def z_plus(k):
        return lax.rem(z_now + k + 8, 8)

    def z_dev(z):
        return (lax.rem(z, 4), fsdp_of(yc, z // 4, xc))

    z_peers = [z_dev(z_plus(k)) for k in range(1, 8)]
    z_side = [z_dev(z_plus(1)), z_dev(z_plus(-1))]
    at_cut = lax.rem(zl, 3) == 0
    outward = 2 * (zl // 2) - 1
    outer, inner = z_dev(z_plus(outward)), z_dev(z_plus(-outward))

    def plane_plus(k):
        return lax.rem(yc * 4 + xc + k, 16)

    def plane_dev(i):
        return (zl, fsdp_of(i // 4, zh, lax.rem(i, 4)))

    plane_peers = [plane_dev(plane_plus(k)) for k in range(1, 16)]

    z_in = pltpu.make_async_copy(z_hbm, z_ref, in_sem.at[0])
    x_in = pltpu.make_async_copy(x_hbm, x_ref, in_sem.at[1])
    z_in.start()
    x_in.start()

    barrier = pltpu.get_barrier_semaphore()
    for dev in [partner] + plane_peers + z_peers:
        pl.semaphore_signal(barrier, inc=1, device_id=dev, device_id_type=MESH)

    def place(t):
        h = lax.rem(1 - zh + t // 16, 2)
        return lax.rem(t // 4, 4), h, lax.rem(t, 4)

    def tok_cols(t, side):
        y, h, x = place(t)
        src = pl.multiple_of((2 * ((y * 2 + h) * 4 + x) + side) * 128, 128)
        dst = pl.multiple_of((h * 4 + x) * 128, 128)
        return y, src, dst

    def local_tok(t):
        y, src, dst = tok_cols(t, core)
        return pltpu.make_async_copy(
            tokens.at[:, pl.ds(src, 128)], tok.at[y, 0, :, pl.ds(dst, 128)], tok_local.at[t]
        )

    def remote_tok(t):
        y, src, dst = tok_cols(t, 1 - core)
        return pltpu.make_async_remote_copy(
            src_ref=tokens.at[:, pl.ds(src, 128)],
            dst_ref=tok.at[y, 1, :, pl.ds(dst, 128)],
            send_sem=tok_send.at[t],
            recv_sem=tok_recv.at[t],
            device_id=partner,
            device_id_type=MESH,
        )

    cot_local = pltpu.make_async_copy(cot_hbm, cot.at[0], in_sem.at[2])
    cot_local.start()

    @pl.loop(0, 32)
    def _(t):
        local_tok(t).start()

    z_in.wait()
    x_in.wait()
    blended = (1.0 - beta_first) * z_ref[...] + beta_first * x_ref[...]
    wts[yc, zh, xc] = blended.astype(BF16)

    pl.semaphore_wait(barrier, 23)

    sends = []
    counter = [0]

    def message(src, dst, dev):
        m = counter[0]
        counter[0] += 1
        copy = pltpu.make_async_remote_copy(
            src_ref=src, dst_ref=dst, send_sem=send_sem.at[m], recv_sem=recv_sem.at[m],
            device_id=dev, device_id_type=MESH,
        )
        copy.start()
        sends.append(copy)
        return m

    def arrived(m, dst):
        pltpu.make_async_remote_copy(
            src_ref=dst, dst_ref=dst, send_sem=send_sem.at[m], recv_sem=recv_sem.at[m],
            device_id=partner, device_id_type=MESH,
        ).wait_recv()

    first = (xc, yc)
    second = (yc, xc)
    first_side = (x_side, y_side)
    second_side = (y_side, x_side)

    def block(p, f, s, h, r0, rows):
        y, x = (s, f) if p == 0 else (f, s)
        return wts.at[y, h, x, pl.ds(r0, rows), :]

    half_of = (zh, 1 - zh)
    ag = {}

    def spread(st, p, item):
        h = half_of[st]
        blk = block(p, mod4(first[p] + item), second[p], h, 64 * p, 64)
        for d in (0, 1):
            ag[st, p, 2, item, d] = message(blk, blk, second_side[p][d])

    def ag0(st):
        h = half_of[st]
        for p in (0, 1):
            own = block(p, first[p], second[p], h, 64 * p, 64)
            for d in (0, 1):
                ag[st, p, 0, d] = message(own, own, first_side[p][d])
    def spread_own(st):
        for p in (0, 1):
            spread(st, p, 0)

    def spread_next(st):
        for p in (0, 1):
            for item in (-1, 1):
                spread(st, p, item)

    def ag1(st):
        h = half_of[st]
        for p in (0, 1):
            f, s, r0 = first[p], second[p], 64 * p
            for d in (0, 1):
                src_f = mod4(f - 1 + 2 * d)
                arrived(ag[st, p, 0, d], block(p, src_f, s, h, r0, 64))
                part = block(p, src_f, s, h, r0 + 32 * d, 32)
                ag[st, p, 1, d] = message(part, part, first_side[p][d])

    def ag2(st):
        h = half_of[st]
        for p in (0, 1):
            f, s, r0 = first[p], second[p], 64 * p
            for d in (0, 1):
                arrived(ag[st, p, 1, d], block(p, mod4(f + 2), s, h, r0 + 32 * d, 32))
            spread(st, p, 2)

    def ag3(st, items):
        h = half_of[st]
        for item in items:
            for p in (0, 1):
                f, s, r0 = first[p], second[p], 64 * p
                for d in (0, 1):
                    src_s = mod4(s - 1 + 2 * d)
                    arrived(ag[st, p, 2, item, d], block(p, mod4(f + item), src_s, h, r0, 64))
                    part = block(p, mod4(f + item), src_s, h, r0 + 32 * d, 32)
                    ag[st, p, 3, item, d] = message(part, part, second_side[p][d])

    def ag4(st):
        h = half_of[st]
        for item in (0, -1, 1, 2):
            for p in (0, 1):
                f, s, r0 = first[p], second[p], 64 * p
                for d in (0, 1):
                    arrived(ag[st, p, 3, item, d], block(p, mod4(f + item), mod4(s + 2), h, r0 + 32 * d, 32))

    zc = {}

    starts = [sum(CHUNKS[:c]) for c in range(len(CHUNKS))]
    chunk = [chunk_refs[6 * c:6 * c + 6] for c in range(len(CHUNKS))]

    def c_row(z, c):
        return pl.ds(pl.multiple_of(lax.rem(z, 4) * C_ROWS + starts[c], 16), CHUNKS[c])

    def zc1(c):
        dest = z_plus(4)
        for d in (0, 1):
            half = gt.at[:, dest // 4, pl.ds(2 * d, 2), c_row(dest, c), :]
            zc[1, d, c] = message(half, chunk[c][0].at[d], z_side[d])

    def zc_step(s, c):
        zc_half, zc_recv, zc_stage = chunk[c][:3]
        for d in (0, 1):
            dest = z_plus((5 - s) * (1 - 2 * d))
            h, row = dest // 4, c_row(dest, c)
            if s == 2:
                arrived(zc[1, d, c], zc_half.at[d])

                @pl.loop(0, 8)
                def _(i):
                    y, x = i // 2, lax.rem(i, 2)
                    mine = gt[y, h, 2 * d + x, row, :].astype(F32)
                    got = zc_half[d, y, x].astype(F32)
                    zc_stage[0, d, y, 2 * d + x] = (mine + got).astype(BF16)
                    other = 2 * (1 - d) + x
                    zc_stage[0, d, y, other] = gt[y, h, other, row, :]
            else:
                arrived(zc[s - 1, d, c], zc_recv.at[s - 3, d])

                @pl.loop(0, 16)
                def _(i):
                    y, x = i // 4, lax.rem(i, 4)
                    mine = gt[y, h, x, row, :].astype(F32)
                    got = zc_recv[s - 3, d, y, x].astype(F32)
                    zc_stage[s - 2, d, y, x] = (mine + got).astype(BF16)

            zc[s, d, c] = message(zc_stage.at[s - 2, d], zc_recv.at[s - 2, d], z_side[d])

    def zc_final(c):
        _, zc_recv, _, c_f, c_b, _ = chunk[c]
        for d in (0, 1):
            arrived(zc[4, d, c], zc_recv.at[2, d])
        row = c_row(z_now, c)

        @pl.loop(0, 16)
        def _(i):
            y, x = i // 4, lax.rem(i, 4)
            total = (
                gt[y, zh, x, row, :].astype(F32)
                + zc_recv[2, 0, y, x].astype(F32)
                + zc_recv[2, 1, y, x].astype(F32)
            )
            c_f[y, x] = total
            c_b[y, x] = total.astype(BF16)

    c_msgs = {}
    shares = {}

    def c_send(c):
        c_b, c_recv = chunk[c][4:]
        for k in range(1, 16):
            i = plane_plus(k)
            c_msgs[c, k] = message(c_b.at[i // 4, lax.rem(i, 4)], c_recv.at[k - 1], plane_peers[k - 1])

    def c_end(c):
        c_f, _, c_recv = chunk[c][3:]
        total = c_f[yc, xc]
        for k in range(1, 16):
            arrived(c_msgs[c, k], c_recv.at[k - 1])
            total = total + c_recv[k - 1].astype(F32)
        gfull[c_row(z_now, c), :] = total
        share(c)

    def nxt(c, d):
        return mod4(c + 1 - 2 * d)

    class Plane:
        def __init__(self, pick, load, bufs):
            self.pick, self.load, self.bufs, self.m = pick, load, bufs, {}

        def start(self, p, which):
            rel, dirc = self.bufs[0], self.bufs[1]
            for d in (0, 1):
                if which == 0:
                    src, dst = self.pick(p, mod4(first[p] + 2), d), rel.at[p, d]
                else:
                    src, dst = self.pick(p, nxt(first[p], d), 1 - d), dirc.at[p, d]
                self.m[p, which, d] = message(src, dst, first_side[p][d])

        def mid(self, p):
            rel, _, summed, stage = self.bufs[:4]
            for d in (0, 1):
                arrived(self.m[p, 0, d], rel.at[p, d])

                @pl.loop(0, 4)
                def _(i):
                    stage[p, d, i] = (self.load(p, nxt(first[p], d), d, i) + rel[p, d, i].astype(F32)).astype(BF16)

                self.m[p, 2, d] = message(stage.at[p, d], summed.at[p, d], first_side[p][d])

        def turn(self, p):
            _, dirc, summed, _, gf, gb, rel2 = self.bufs[:7]
            for d in (0, 1):
                arrived(self.m[p, 1, d], dirc.at[p, d])
                arrived(self.m[p, 2, d], summed.at[p, d])
            for h in (0, 1):
                @pl.loop(0, 4)
                def _(i):
                    total = (
                        self.load(p, first[p], h, i)
                        + dirc[p, 1 - h, i].astype(F32)
                        + summed[p, h, i].astype(F32)
                    )
                    gf[p, i, h] = total
                    gb[p, i, h] = total.astype(BF16)
            for d in (0, 1):
                src = gb.at[p, mod4(second[p] + 2), d]
                self.m[p, 3, d] = message(src, rel2.at[p, d], second_side[p][d])

        def turn2(self, p):
            gb, _, dir2 = self.bufs[5:8]
            for d in (0, 1):
                src = gb.at[p, nxt(second[p], d), 1 - d]
                self.m[p, 4, d] = message(src, dir2.at[p, d], second_side[p][d])

        def mid2(self, p):
            gf, _, rel2, _, summed2, stage2_ = self.bufs[4:]
            for d in (0, 1):
                arrived(self.m[p, 3, d], rel2.at[p, d])
                stage2_[p, d] = (gf[p, nxt(second[p], d), d] + rel2[p, d].astype(F32)).astype(BF16)
                self.m[p, 5, d] = message(stage2_.at[p, d], summed2.at[p, d], second_side[p][d])

        def end(self, p):
            gf, _, _, dir2, summed2, _ = self.bufs[4:]
            for d in (0, 1):
                arrived(self.m[p, 4, d], dir2.at[p, d])
                arrived(self.m[p, 5, d], summed2.at[p, d])
            return [
                gf[p, second[p], h] + dir2[p, 1 - h].astype(F32) + summed2[p, h].astype(F32)
                for h in (0, 1)
            ]

    def ab_pick(p, f, h):
        rows = pl.ds(AB + R * p, R)
        return gt.at[:, h, f, rows, :] if p == 0 else gt.at[f, h, :, rows, :]

    def ab_load(p, f, h, i):
        rows = pl.ds(AB + R * p, R)
        return (gt[i, h, f, rows, :] if p == 0 else gt[f, h, i, rows, :]).astype(F32)

    ab = Plane(ab_pick, ab_load, (relay1, direct1, summed1, stage1, g1f, g1b, relay2, direct2, summed2, stage2))

    def grad(j0, j1):
        @pl.loop(j0, j1)
        def _(j):
            for t in (2 * j, 2 * j + 1):
                local_tok(t).wait()
                remote_tok(t).wait_recv()
            y, h, x = place(2 * j)
            col = pl.multiple_of(h * 512 + x * 128, 256)
            rhs = tok[y, :, :, pl.ds(col, 256)].reshape(1024, 256)
            for q in (0, 1):
                rows = slice(256 * q, 256 * (q + 1))
                out = jnp.dot(cot_t[rows, :], rhs, preferred_element_type=F32).astype(BF16)
                gt[y, h, x, rows, :] = out[:, :128]
                gt[y, h, x + 1, rows, :] = out[:, 128:]

    def values(st, y, m):
        h = half_of[st]
        lhs = tok[y, m, :, pl.ds(pl.multiple_of(h * 512, 512), 512)]
        out = jnp.dot(lhs, wts[y, h].reshape(512, 512), preferred_element_type=F32)
        acc[m] = out if (st, y) == (0, 0) else acc[m] + out

    def values2(st, y, m):
        h = half_of[st]
        cols = pl.ds(pl.multiple_of(h * 512, 512), 512)
        total = acc[m]
        for k in (0, 1):
            rhs = wts[y + k, h].reshape(512, 512)
            total = total + jnp.dot(tok[y + k, m, :, cols], rhs, preferred_element_type=F32)
        acc[m] = total

    def z_send():
        out = []
        for k in range(1, 8):
            dest = z_plus(k)
            part = zstage.at[dest // 4, pl.ds(pl.multiple_of(lax.rem(dest, 4) * Q, 16), Q), :]
            out.append(message(part, zrecv.at[k - 1], z_peers[k - 1]))
        return out

    def z_end(msgs):
        total = plane[zh, pl.ds(pl.multiple_of(zl * Q, 16), Q), :]
        for k in range(7):
            arrived(msgs[k], zrecv.at[k])
            total = total + zrecv[k].astype(F32)
        gfull[rows_of(zl, "ab"), :] = total
        share("ab")

    def rows_of(z, part):
        if part == "ab":
            return pl.ds(pl.multiple_of(AB + lax.rem(z, 4) * Q, 16), Q)
        return c_row(z, part)

    def share(part):
        rows = gfull.at[rows_of(zl, part), :]
        for k in range(1, 4):
            shares[part, k] = message(rows, rows, (lax.rem(zl + k, 4), index))

    def shared(part):
        for k in range(1, 4):
            arrived(shares[part, k], gfull.at[rows_of(zl + 4 - k, part), :])

    def cut_copy(n, src, dev):
        m = N_MSG - 2 + n
        return pltpu.make_async_remote_copy(
            src_ref=src, dst_ref=src, send_sem=send_sem.at[m], recv_sem=recv_sem.at[m],
            device_id=dev, device_id_type=MESH,
        )

    own_block = wts.at[yc, zh, xc]
    other_block = wts.at[yc, 1 - zh, xc]

    def cut_send():
        @pl.when(at_cut)
        def _():
            cut_copy(0, own_block, outer).start()

    def cut_forward():
        @pl.when(at_cut)
        def _():
            cut_copy(0, other_block, outer).wait_recv()
            cut_copy(1, other_block, inner).start()

    def cut_end():
        @pl.when(jnp.logical_not(at_cut))
        def _():
            cut_copy(1, other_block, outer).wait_recv()

    def ab_start(which):
        for p in (0, 1):
            ab.start(p, which)

    def ab_all(step):
        for p in (0, 1):
            step(p)

    def ab_end():
        for p in (0, 1):
            for h, total in enumerate(ab.end(p)):
                plane[h, R * p:R * (p + 1), :] = total
                zstage[h, R * p:R * (p + 1), :] = total.astype(BF16)

    def finish_sends(lo, hi):
        for copy in sends[lo:hi]:
            copy.wait_send()

    def finish_early():
        finish_sends(0, early)

        @pl.when(at_cut)
        def _():
            cut_copy(0, own_block, outer).wait_send()
            cut_copy(1, other_block, inner).wait_send()

        @pl.loop(0, 32)
        def _(t):
            remote_tok(t).wait_send()

    cot_msg = message(cot_hbm, cot.at[1], partner)
    ag0(0)
    cut_send()

    @pl.loop(0, 32)
    def _(t):
        remote_tok(t).start()

    cot_local.wait()
    cot_t[:, :512] = cot[0].T
    arrived(cot_msg, cot.at[1])
    cot_t[:, 512:] = cot[1].T
    spread_own(0)
    grad(0, 2)
    grad(2, 4)
    grad(4, 6)
    grad(6, 8)
    zc1(1)
    ag1(0)
    spread_next(0)
    zc1(0)
    grad(8, 10)
    grad(10, 12)
    grad(12, 14)
    grad(14, 16)
    ab_start(0)
    cut_forward()
    ag2(0)
    zc_step(2, 1)
    ag3(0, (0,))
    ab_start(1)
    zc_step(2, 0)
    ag3(0, (-1, 1))
    ag3(0, (2,))
    cut_end()
    ag0(1)
    spread_own(1)
    ab_all(ab.mid)
    zc_step(3, 1)
    ag4(0)
    values(0, 0, 0)
    values(0, 0, 1)
    values(0, 1, 0)
    zc_step(3, 0)
    values(0, 1, 1)
    values(0, 2, 0)
    values(0, 2, 1)
    values(0, 3, 0)
    values(0, 3, 1)
    ag3(1, (0,))
    ag1(1)
    spread_next(1)
    ab_all(ab.turn)
    ab_all(ab.turn2)
    zc_step(4, 1)
    ag2(1)
    zc_step(4, 0)
    ab_all(ab.mid2)
    zc_final(1)
    c_send(1)
    ag3(1, (-1, 1))
    ag3(1, (2,))
    ab_end()
    z_msgs = z_send()
    zc_final(0)
    c_send(0)
    c_end(1)
    ag4(1)
    values2(1, 0, 1)
    z_end(z_msgs)
    values2(1, 2, 1)
    vmsg = message(acc.at[1], vrecv, partner)
    values2(1, 0, 0)
    c_end(0)
    values2(1, 2, 0)
    early = counter[0] - 30
    finish_early()
    arrived(vmsg, vrecv)
    values_out[...] = ((acc[0] + vrecv[...]) * NORM).astype(BF16)
    for part in (*range(2), "ab"):
        shared(part)
    grad_out[...] = gfull[...]

    finish_sends(early, len(sends))

    assert counter[0] <= N_MSG - 2


def finish(values_ref, grad_ref, z_ref, x_ref, s_ref, values_out, z_out, x_out, s_out):
    values_out[...] = values_ref[...]
    gradient = grad_ref[...].T * NORM
    z_in = z_ref[...]
    x_in = x_ref[...]
    mixed = (1.0 - beta_first) * z_in + beta_first * x_in
    second_next = beta_second * s_ref[...] + (1.0 - beta_second) * gradient * gradient
    scaled = gradient / (jnp.sqrt(second_next / bias_fix) + epsilon)
    z_next = z_in - learn_rate * (scaled + weight_decay * mixed)
    s_out[...] = second_next
    z_out[...] = z_next
    x_out[...] = (1.0 - mixing) * x_in + mixing * z_next


def local(tokens, cotangent, z_weights, x_weights, second_moment):
    vm = pl.BlockSpec(memory_space=pltpu.VMEM)
    hbm = pl.BlockSpec(memory_space=pl.ANY)
    shard = jax.ShapeDtypeStruct((128, HV), F32)
    vals = jax.ShapeDtypeStruct((TOK, HV), BF16)
    dma = pltpu.SemaphoreType.DMA

    def plane_bufs(r):
        return (
            [pltpu.VMEM((2, 2, 4, r, 128), BF16)] * 4
            + [pltpu.VMEM((2, 4, 2, r, 128), F32), pltpu.VMEM((2, 4, 2, r, 128), BF16)]
            + [pltpu.VMEM((2, 2, r, 128), BF16)] * 4
        )

    def chunk_bufs(r):
        return [
            pltpu.VMEM((2, 4, 2, r, 128), BF16),
            pltpu.VMEM((3, 2, 4, 4, r, 128), BF16),
            pltpu.VMEM((3, 2, 4, 4, r, 128), BF16),
            pltpu.VMEM((4, 4, r, 128), F32),
            pltpu.VMEM((4, 4, r, 128), BF16),
            pltpu.VMEM((15, r, 128), BF16),
        ]

    values, gradient = pl.pallas_call(
        kernel,
        out_shape=(vals, jax.ShapeDtypeStruct((HV, 128), F32)),
        in_specs=[hbm, hbm, hbm, hbm],
        out_specs=(vm, vm),
        scratch_shapes=[
            pltpu.VMEM((128, HV), F32),
            pltpu.VMEM((128, HV), F32),
            pltpu.VMEM((4, 2, 512, 1024), BF16),
            pltpu.VMEM((2, 512, 512), BF16),
            pltpu.VMEM((512, 1024), BF16),
            pltpu.VMEM((4, 2, 4, 128, 512), BF16),
            pltpu.VMEM((4, 2, 4, 512, 128), BF16),
        ] + plane_bufs(R) + [
            pltpu.VMEM((2, 2 * R, 128), F32),
            pltpu.VMEM((2, 2 * R, 128), BF16),
            pltpu.VMEM((7, Q, 128), BF16),
            pltpu.VMEM((512, 128), F32),
            pltpu.VMEM((2, 512, 512), F32),
            pltpu.VMEM((512, 512), F32),
            dma((N_MSG,)),
            dma((N_MSG,)),
            dma((32,)),
            dma((32,)),
            dma((32,)),
            dma((3,)),
        ] + [ref for r in CHUNKS for ref in chunk_bufs(r)],
        compiler_params=pltpu.CompilerParams(
            collective_id=0, has_side_effects=True, vmem_limit_bytes=48 * 1024 * 1024
        ),
    )(tokens, *[pltpu.with_memory_space_constraint(a, pltpu.HBM) for a in (cotangent, z_weights, x_weights)])
    return pl.pallas_call(
        finish,
        out_shape=(vals, shard, shard, shard),
        in_specs=[vm] * 5,
        out_specs=(vm,) * 4,
        compiler_params=pltpu.CompilerParams(vmem_limit_bytes=12 * 1024 * 1024),
    )(values, gradient, z_weights, x_weights, second_moment)


def solution(mesh):
    return jax.shard_map(
        local,
        mesh=mesh,
        in_specs=(
            P(("replica", "fsdp"), None),
            P(("replica", "fsdp"), None),
            P("fsdp", None),
            P("fsdp", None),
            P("fsdp", None),
        ),
        out_specs=(P(("replica", "fsdp"), None), P("fsdp", None), P("fsdp", None), P("fsdp", None)),
        check_vma=False,
    )
```
